512 devices in a mesh: ka: 64 (over x, y, core), ta: 8 (over z).
Axes of the slice: x: 4, y: 8, z: 8, core: 2. Of those that a mesh axis runs over, the one named last changes fastest.
Arguments:
- sigma_history: bfloat16 [128, 4096, 256], P('ka', 'ta'), may hold values from -6 to 6
- time_basis: bfloat16 [4096, 64], P('ta'), may hold values from -0.75 to 0.75
- history_coef: bfloat16 [128, 512, 256], P('ka', 'ta'), may hold values from -6 to 6
- green_now: float32 [128, 256], P('ka'), may hold values from -6 to 6
- hamilton: float32 [128, 256], P('ka'), may hold values from -1.5 to 1.5
- panel_block: bfloat16 [128, 2048, 2048], P('ka', 'ta'), may hold values from -7 to 7
- panel_lengths: int32 [8], P('ta'), may hold values from 1 to 16, 120 in all
- owners: int32 [128, 1], P('ka'), may hold values from 0 to 15
- sketch: bfloat16 [16, 2048, 64], P(None, 'ka'), may hold values from -6 to 6
Outputs:
- green_next: float32 [128, 256], P('ka')
- ortho_factor: float32 [128, 2048, 64], P('ka', 'ta')
- coef_factor: float32 [128, 64, 2048], P('ka', None, 'ta')
The draws below stay inside these ranges and needn't reach their ends.
Inputs may be any that keep to these rules, and one draw needn't show every extreme that they name: `owners`: every compressor rank serves some k-point. `panel_lengths`: they sum to 120; the largest is 16.
All inputs are finite; a program needn't handle non-finite values. No bound on the sum of `panel_lengths` on one device may be relied on, other than what follows from the above.
Results may differ from the reference program's by a relative error of at most 0.0095.
Values may be sent and summed in bfloat16 or wider, within the bound.
No kernel may reach another device: no remote copies, remote signals or barrier semaphores. Data moves between devices by JAX's collectives and lax.ppermute only.
A program may use at most 64 MiB of HBM per device.

```python
import math
import jax
import jax.numpy as jnp
import numpy as np
from jax import lax

NO = 16
OO = 256
R = 64
HIST_DEV = 512
PROW_DEV = 16
NCMP = 16
KPTS = 128
HORIZON = 4096
NTB = 8
RB = 512
PROWS = 2048
PCOLS = 2048
TOTAL = 120
N_TA = 8


def draw_panel_block(key, part):
    shape = (KPTS, PROWS, PCOLS)
    values = jax.random.normal(jax.random.fold_in(key, 12), shape, jnp.float32)
    return jnp.clip(values, -6.0, 6.0).astype(jnp.bfloat16)


def draw_sketch(key, part):
    shape = (NCMP, PCOLS, R)
    values = jax.random.normal(jax.random.fold_in(key, 22), shape, jnp.float32)
    return jnp.clip(values, -6.0, 6.0).astype(jnp.bfloat16)


def block_levels(key, dims, cuts, smallest, top_value):
    loudness, own = 1.0, jax.random.fold_in(key, 6)
    for dim, shards_of in cuts:
        draws = jnp.exp(jax.random.uniform(jax.random.fold_in(own, dim), (shards_of,), jnp.float32, smallest / len(cuts), top_value / len(cuts)))
        loudness = loudness * jnp.repeat(draws, dims[dim] // shards_of).reshape([-1 if axis == dim else 1 for axis in range(len(dims))])
    return loudness


def picks_of(stream_key, rows, count, top, lift):
    ranking = jax.random.permutation(jax.random.fold_in(stream_key, 1), count)
    boost = ranking
    for power in range(3):
        boost = boost * boost // count
    boost = boost * lift // count
    tickets = jax.random.randint(jax.random.fold_in(stream_key, 2), (rows, count), 0, 4096) + boost
    sure = jax.random.permutation(jax.random.fold_in(stream_key, 3), rows)[jnp.arange(count) % rows]
    tickets = jnp.where(jnp.arange(rows)[:, None] == sure[None, :], 1 << 14, tickets)
    score = tickets * count + jnp.arange(count)
    return lax.top_k(score.astype(jnp.int32), top)[1].astype(jnp.int32)


def length_profile(amount, total, limit, skew):
    weights = [(1 << 20) // math.isqrt(rank ** skew) + 1 for rank in range(2, amount + 1)]
    surplus, counts = total - limit - (amount - 1), [1] * (amount - 1)
    while surplus > 0:
        movable = [i for i in range(amount - 1) if counts[i] < limit]
        mass, left = sum([weights[i] for i in movable]), surplus
        for i in movable:
            more = min(limit - counts[i], max(1, left * weights[i] // mass), surplus)
            counts[i] = counts[i] + more
            surplus = surplus - more
    return np.array([limit] + counts)


def uneven(stream_key, number_of, total, bound, lean):
    if number_of == 2:
        one = jax.random.randint(stream_key, (), max(1, total - bound), min(bound, total - 1) + 1)
        return jnp.stack([one, total - one])
    lengths = jnp.asarray(length_profile(number_of, total, bound, lean), jnp.int32)
    couples = (number_of - 1) // 2
    donor, sink = lengths[1:1 + 2 * couples:2], lengths[2:2 + 2 * couples:2]
    room = jnp.minimum(donor - 1, bound - sink)
    passed = jax.random.randint(jax.random.fold_in(stream_key, 1), (couples,), 0, 1 << 20) % (room + 1)
    lengths = lengths.at[1:1 + 2 * couples:2].set(donor - passed).at[2:2 + 2 * couples:2].set(sink + passed)
    return lengths[jax.random.permutation(jax.random.fold_in(stream_key, 2), number_of)]


def scatter_about(stream_key, shape, width, most, pieces=(), kind=jnp.bfloat16):
    drawn = jax.random.normal(stream_key, shape, jnp.float32) * width
    if len(pieces) > 0:
        drawn = block_levels(stream_key, shape, pieces, -0.22, 0.18) * drawn
    return jnp.clip(drawn, min=-most, max=most).astype(kind)


def setup_inputs(seed: int = 0) -> dict:
    splits = jax.random.split(jax.random.key(seed), 10)
    return {
        "sigma_history": scatter_about(splits[0], (KPTS, HORIZON, OO), 1.0, 6.0, ((0, 64), (1, 8))),
        "time_basis": scatter_about(splits[1], (HORIZON, R), R ** -0.5, 0.75, ((0, 8),)),
        "history_coef": scatter_about(splits[2], (KPTS, RB, OO), 1.0, 6.0, ((0, 64), (1, 8))),
        "green_now": scatter_about(splits[3], (KPTS, OO), 1.0, 6.0, ((0, 64),), jnp.float32),
        "hamilton": scatter_about(splits[4], (KPTS, OO), 0.25, 1.5, ((0, 64),), jnp.float32),
        "panel_block": draw_panel_block(jax.random.fold_in(splits[9], 71), 0),
        "panel_lengths": uneven(splits[6], NTB, TOTAL, PROW_DEV, 2).astype(jnp.int32),
        "owners": picks_of(splits[7], KPTS, NCMP, 1, 1024),
        "sketch": draw_sketch(jax.random.fold_in(splits[9], 71), 0),
    }


step_size = 0.25

def reference(sigma_history, time_basis, history_coef, green_now, hamilton, panel_block, panel_lengths, owners, sketch):
    high = lax.Precision.HIGHEST

    def block_term(carry, block_index):
        sigma_block = lax.dynamic_slice_in_dim(sigma_history, block_index * HIST_DEV, HIST_DEV, 1).astype(jnp.float32)
        basis_block = lax.dynamic_slice_in_dim(time_basis, block_index * HIST_DEV, HIST_DEV, 0).astype(jnp.float32)
        coef_block = lax.dynamic_slice_in_dim(history_coef, block_index * R, R, 1).astype(jnp.float32)
        summed = jnp.einsum('jr,kjo->kro', basis_block, sigma_block, precision=high).reshape(KPTS, R, NO, NO)
        coef_block = coef_block.reshape(KPTS, R, NO, NO)
        return (carry + jnp.einsum('krac,krcd->kad', summed, coef_block, precision=high), None)
    blocks = jnp.arange(N_TA, dtype=jnp.int32)
    total_term, unused = lax.scan(block_term, jnp.zeros((KPTS, NO, NO), jnp.float32), blocks)
    integral = total_term / jnp.sqrt(jnp.float32(NO * HORIZON))
    green = green_now.reshape(KPTS, NO, NO)
    hmat = hamilton.reshape(KPTS, NO, NO)
    for repeat in range(2):
        left_prod = jnp.einsum('kac,kcd->kad', hmat, green, precision=high)
        right_prod = jnp.einsum('kac,kcd->kad', green, hmat, precision=high)
        green = green + step_size * (left_prod - right_prod + integral)
    green_next = green.reshape(KPTS, NO * NO)
    starts = jnp.cumsum(panel_lengths) - panel_lengths
    slot_index = jnp.arange(PROW_DEV, dtype=jnp.int32)
    row_time = starts[:, None] + slot_index[None, :]
    row_live = slot_index[None, :] < panel_lengths[:, None]
    col_time = jnp.arange(PCOLS, dtype=jnp.int32) // NO - PROW_DEV // 2
    keep = row_live[:, :, None, None] & (col_time[None, None, None, :] <= row_time[:, :, None, None])
    keep = jnp.broadcast_to(keep, (N_TA, PROW_DEV, NO, PCOLS)).reshape(PROWS, PCOLS)
    masked = jnp.where(keep[None], panel_block, jnp.zeros_like(panel_block))
    omega = jnp.take(sketch, owners[:, 0], axis=0)
    sketched = jnp.einsum('krx,kxq->krq', masked.astype(jnp.float32), omega.astype(jnp.float32), precision=high)
    gram = jnp.einsum('krq,krp->kqp', sketched, sketched, precision=high)
    lower = jnp.linalg.cholesky(gram)
    ortho = lax.linalg.triangular_solve(lower, sketched, left_side=False, lower=True, transpose_a=True)
    rounded = lax.optimization_barrier(ortho.astype(jnp.bfloat16)).astype(jnp.float32)
    rounded_blocks = rounded.reshape(KPTS, N_TA, PROW_DEV * NO, R)
    masked_blocks = masked.astype(jnp.float32).reshape(KPTS, N_TA, PROW_DEV * NO, PCOLS)
    partial_terms = jnp.einsum('kbrq,kbrc->kbqc', rounded_blocks, masked_blocks, precision=high)
    partial_terms = lax.optimization_barrier(partial_terms.astype(jnp.bfloat16)).astype(jnp.float32)
    coef_factor = lax.optimization_barrier(jnp.sum(partial_terms, axis=1))
    return (green_next, ortho, coef_factor)
```

```python
import jax
import jax.numpy as jnp
from jax import lax
from jax.experimental import pallas as pl
from jax.experimental.pallas import tpu as pltpu
from jax.sharding import PartitionSpec as P

NO = 16
OO = NO * NO
R = 64
SLOTS = 16
LANES = 128
STEP = 0.25
HIGH = lax.Precision.HIGHEST
F32 = jnp.float32
BF16 = jnp.bfloat16


def dot(left, right, contract, precision=None):
    return lax.dot_general(
        left, right, (contract, ((), ())), precision=precision, preferred_element_type=F32
    )


def iota(shape, dim):
    return lax.broadcasted_iota(jnp.int32, shape, dim)


def pick_rows(ka_count, ta_count, told, sketch):
    def kernel(told, me, sketch, picked, facts, double):
        for rank in range(sketch.shape[0]):
            rows = sketch[rank]
            double[rank] = jnp.concatenate([rows, rows], axis=1)
        left = iota(double.shape[1:], 1) < R

        def one(place, carry):
            picked[place] = jnp.where(left, double[told[place, 0]], double[told[place, 1]])
            return carry

        lax.fori_loop(0, ka_count, one, 0, unroll=8)
        begin = jnp.int32(0)
        length = jnp.int32(0)
        for place in range(ta_count):
            where_from, amount = told[place, 3], told[place, 2]
            begin = begin + jnp.where(where_from < me[0], amount, 0)
            length = length + jnp.where(where_from == me[0], amount, 0)
        facts[0] = begin
        facts[1] = length

    ranks, rows, _ = sketch.shape
    smem = pl.BlockSpec(memory_space=pltpu.SMEM)
    vmem = pl.BlockSpec(memory_space=pltpu.VMEM)
    me = lax.axis_index("ta").astype(jnp.int32).reshape(1)
    return pl.pallas_call(
        kernel,
        out_shape=(
            jax.ShapeDtypeStruct((ka_count, rows, LANES), BF16),
            jax.ShapeDtypeStruct((2,), jnp.int32),
        ),
        in_specs=[smem, smem, vmem],
        out_specs=(vmem, smem),
        scratch_shapes=[pltpu.VMEM((ranks, rows, LANES), BF16)],
        compiler_params=pltpu.CompilerParams(vmem_limit_bytes=8 << 20),
        name="pick_rows",
    )(told, me, sketch)


def keep_mask(facts, rows, cols):
    slot = iota((rows, 1), 0) >> 4
    top = jnp.where(slot < facts[1], facts[0] + slot + SLOTS // 2, -1)
    group = iota((1, cols), 1) >> 4
    return group.astype(F32).astype(BF16) <= top.astype(F32).astype(BF16)


def sketch_panels(facts, chosen, panel, sigma, basis, coef, copies):
    def kernel(facts, chosen, panel, sigma, basis, coef, sketched, shared):
        k_count, rows, cols = panel.shape
        keep = keep_mask(facts, rows, cols)
        zero = jnp.zeros((rows, cols), BF16)
        parts = [
            dot(jnp.where(keep, panel[k], zero), chosen[...], ((1,), (0,))) for k in range(k_count)
        ]
        both = jnp.where(iota((rows, LANES), 1) < R, parts[0], parts[1])
        sketched[...] = both
        square = dot(both, both, ((0,), (0,)), HIGH)
        gram = jnp.where(iota((R, LANES), 1) < R, square[:R], square[R:])

        row, col = iota((OO, OO), 0), iota((OO, OO), 1)
        inner = (row & 15) == (col >> 4)
        spread = jnp.where((row & 15) == (col & 15), 1.0, 0.0).astype(F32)
        same = (row >> 4) == (col >> 4)
        lines = []
        for k in range(k_count):
            summed = dot(basis[...], sigma[k], ((1,), (0,)))
            pairs = dot(summed, coef[k].astype(F32), ((0,), (0,)), HIGH)
            laid = dot(jnp.where(inner, pairs, 0.0), spread, ((1,), (0,)), HIGH)
            line = jnp.sum(jnp.where(same, laid, 0.0), axis=0, keepdims=True)
            lines += [line[:, :LANES], line[:, LANES:]]
        tail = jnp.concatenate(lines + [jnp.zeros((4, LANES), F32)], axis=0)
        for place in range(copies):
            shared[place, :R] = gram
            shared[place, R:] = tail

    k_count, rows, cols = panel.shape
    smem = pl.BlockSpec(memory_space=pltpu.SMEM)
    vmem = pl.BlockSpec(memory_space=pltpu.VMEM)
    return pl.pallas_call(
        kernel,
        out_shape=(
            jax.ShapeDtypeStruct((rows, LANES), F32),
            jax.ShapeDtypeStruct((copies, R + 8, LANES), F32),
        ),
        in_specs=[smem] + [vmem] * 5,
        out_specs=(vmem, vmem),
        compiler_params=pltpu.CompilerParams(vmem_limit_bytes=20 << 20),
        name="sketch_panels",
    )(facts, chosen, panel, sigma, basis, coef)


def inverse_factor(work, offset):
    lane = iota((R, LANES), 1)
    row = iota((R, 1), 0)
    diag = jnp.zeros((R, 1), F32)
    for step in range(R):
        low = (step // 8) * 8
        part = work[low:]
        line = work[step : step + 1]
        pivot = line[:, offset + step : offset + step + 1]
        scale = part[:, offset + step : offset + step + 1] * (1.0 / pivot)
        scale = jnp.where(row[low:] > step, scale, 0.0)
        diag = jnp.where(row == step, pivot, diag)
        part = part - scale * line
        work = part if low == 0 else jnp.concatenate([work[:low], part], axis=0)
    return work * lax.rsqrt(diag), lane


def finish_panels(facts, told, sketched, panel, green, hamilton, chunk):
    def kernel(facts, told, sketched, panel, green, hamilton, next_green, ortho, terms):
        k_count, rows, cols = panel.shape
        total = told[0]
        for place in range(1, told.shape[0]):
            total = total + told[place]
        gram = total[:R]
        lane = iota((R, LANES), 1)
        left = lane < R
        eye = jnp.where((lane & (R - 1)) == iota((R, LANES), 0), 1.0, 0.0).astype(F32)
        first, _ = inverse_factor(jnp.where(left, gram, eye), 0)
        second, _ = inverse_factor(jnp.where(left, eye, gram), R)
        zero = jnp.zeros((R, LANES), F32)
        factor = jnp.concatenate(
            [
                jnp.where(left, pltpu.roll(first, R, 1), zero),
                jnp.where(left, zero, pltpu.roll(second, R, 1)),
            ],
            axis=0,
        )
        both = dot(factor, sketched[...], ((1,), (1,)), HIGH)
        ortho[0] = both[:R]
        ortho[1] = both[R:]
        rounded = both.astype(BF16)
        keep = keep_mask(facts, rows, cols)
        blank = jnp.zeros((rows, cols), BF16)
        for k in range(k_count):
            coeffs = dot(rounded, jnp.where(keep, panel[k], blank), ((1,), (0,)))
            coeffs = coeffs[k * R : (k + 1) * R].astype(BF16)
            for place in range(cols // chunk):
                for half in range(chunk // LANES):
                    at = place * chunk + half * LANES
                    base = (k * (chunk // LANES) + half) * R
                    terms[place, base : base + R] = coeffs[:, at : at + LANES]

        outer = (iota((NO, OO), 1) >> 4) == iota((NO, OO), 0)
        tile = jnp.where((iota((NO, OO), 1) & 15) == iota((NO, OO), 0), 1.0, 0.0).astype(F32)

        def square(line):
            return dot(jnp.where(outer, line, 0.0), tile, ((1,), (1,)), HIGH)

        for k in range(k_count):
            base = R + 2 * k
            line = jnp.concatenate([total[base : base + 1], total[base + 1 : base + 2]], axis=1)
            rate = square(line) * (1.0 / 256.0)
            g, h = square(green[k : k + 1]), square(hamilton[k : k + 1])
            for _ in range(2):
                left_prod = dot(h, g, ((1,), (0,)), HIGH)
                right_prod = dot(g, h, ((1,), (0,)), HIGH)
                g = g + STEP * (left_prod - right_prod + rate)
            flat = jnp.where(outer, dot(g, tile, ((1,), (0,)), HIGH), 0.0)
            next_green[k : k + 1] = jnp.sum(flat, axis=0, keepdims=True)

    k_count, rows, cols = panel.shape
    smem = pl.BlockSpec(memory_space=pltpu.SMEM)
    vmem = pl.BlockSpec(memory_space=pltpu.VMEM)
    return pl.pallas_call(
        kernel,
        out_shape=(
            jax.ShapeDtypeStruct((k_count, OO), F32),
            jax.ShapeDtypeStruct((k_count, R, rows), F32),
            jax.ShapeDtypeStruct((cols // chunk, k_count * R * chunk // LANES, LANES), BF16),
        ),
        in_specs=[smem] + [vmem] * 5,
        out_specs=(vmem, vmem, vmem),
        compiler_params=pltpu.CompilerParams(vmem_limit_bytes=20 << 20),
        name="finish_panels",
    )(facts, told, sketched, panel, green, hamilton)


def add_terms(told, k_count, chunk):
    def kernel(told, out):
        total = told[0].astype(F32)
        for place in range(1, told.shape[0]):
            total = total + told[place].astype(F32)
        halves = chunk // LANES
        for k in range(k_count):
            for half in range(halves):
                base = (k * halves + half) * R
                out[k, :, half * LANES : (half + 1) * LANES] = total[base : base + R]

    vmem = pl.BlockSpec(memory_space=pltpu.VMEM)
    return pl.pallas_call(
        kernel,
        out_shape=jax.ShapeDtypeStruct((k_count, R, chunk), F32),
        in_specs=[vmem],
        out_specs=vmem,
        compiler_params=pltpu.CompilerParams(vmem_limit_bytes=8 << 20),
        name="add_terms",
    )(told)


def body(
    sigma_history,
    time_basis,
    history_coef,
    green_now,
    hamilton,
    panel_block,
    panel_lengths,
    owners,
    sketch,
):
    ka_count, ta_count = lax.axis_size("ka"), lax.axis_size("ta")
    k_count = green_now.shape[0]
    assert NO * sigma_history.shape[1] * ta_count == 65536 and k_count == 2
    groups = [
        [place * ta_count + (group + place) % ta_count for place in range(ka_count)]
        for group in range(ta_count)
    ]
    facts = jnp.concatenate(
        [owners[:, 0], panel_lengths, lax.axis_index("ta").astype(jnp.int32).reshape(1)]
    )
    facts = jnp.pad(facts, (0, LANES - 4))
    told = lax.all_to_all(
        jnp.broadcast_to(facts[None, None], (ka_count, 1, LANES)),
        ("ka", "ta"),
        0,
        0,
        axis_index_groups=groups,
    ).reshape(ka_count, LANES)
    picked, facts = pick_rows(ka_count, ta_count, told, sketch)
    chosen = lax.all_to_all(picked, "ka", 0, 0).reshape(-1, LANES)
    sketched, shared = sketch_panels(
        facts, chosen, panel_block, sigma_history, time_basis.T, history_coef, ta_count
    )
    told = lax.all_to_all(shared, "ta", 0, 0)
    chunk = panel_block.shape[2] // ta_count
    green_next, ortho, terms = finish_panels(
        facts, told, sketched, panel_block, green_now, hamilton, chunk
    )
    told = lax.all_to_all(terms, "ta", 0, 0)
    return (green_next, ortho.transpose(0, 2, 1), add_terms(told, k_count, chunk))


def solution(mesh):
    in_specs = (
        P("ka", "ta", None),
        P("ta", None),
        P("ka", "ta", None),
        P("ka", None),
        P("ka", None),
        P("ka", "ta", None),
        P("ta"),
        P("ka", None),
        P(None, "ka", None),
    )
    out_specs = (P("ka", None), P("ka", "ta", None), P("ka", None, "ta"))
    return jax.shard_map(body, mesh=mesh, in_specs=in_specs, out_specs=out_specs, check_vma=False)
```

```python
import jax
import jax.numpy as jnp
from jax import lax
from jax.experimental import pallas as pl
from jax.experimental.pallas import tpu as pltpu
from jax.sharding import PartitionSpec as P

NO = 16
OO = NO * NO
R = 64
SLOTS = 16
LANES = 128
STEP = 0.25
BATCH = 4
TOLD = R // 2 + 8
SHIFT = 2.0**-12
TINY = 1e-30
HIGH = lax.Precision.HIGHEST
F32 = jnp.float32
BF16 = jnp.bfloat16


def dot(left, right, contract, precision=None):
    return lax.dot_general(
        left, right, (contract, ((), ())), precision=precision, preferred_element_type=F32
    )


def iota(shape, dim):
    return lax.broadcasted_iota(jnp.int32, shape, dim)


def pick_rows(ka_count, ta_count, told, sketch, bring):
    count = len(bring)

    def kernel(told, me, sketch_far, *refs):
        far, (picked, facts), near = refs[:count], refs[count : count + 2], refs[count + 2 :]
        near, (sketch, double, sem) = near[:count], near[count:]
        load = pltpu.make_async_copy(sketch_far, sketch, sem.at[count])
        load.start()
        loads = [pltpu.make_async_copy(far[i], near[i], sem.at[i]) for i in range(count)]
        for other in loads:
            other.start()
        begin = jnp.int32(0)
        length = jnp.int32(0)
        for place in range(ta_count):
            where_from, amount = told[place, 3], told[place, 2]
            begin = begin + jnp.where(where_from < me[0], amount, 0)
            length = length + jnp.where(where_from == me[0], amount, 0)
        facts[0] = begin
        facts[1] = length
        load.wait()
        for rank in range(sketch.shape[0]):
            rows = sketch[rank]
            double[rank] = jnp.concatenate([rows, rows], axis=1)
        left = iota(double.shape[1:], 1) < R

        def one(place, carry):
            picked[place] = jnp.where(left, double[told[place, 0]], double[told[place, 1]])
            return carry

        lax.fori_loop(0, ka_count, one, 0, unroll=8)
        for other in loads:
            other.wait()

    ranks, rows, _ = sketch.shape
    smem = pl.BlockSpec(memory_space=pltpu.SMEM)
    vmem = pl.BlockSpec(memory_space=pltpu.VMEM)
    hbm = pl.BlockSpec(memory_space=pltpu.HBM)
    me = lax.axis_index("ta").astype(jnp.int32).reshape(1)
    return pl.pallas_call(
        kernel,
        out_shape=(
            jax.ShapeDtypeStruct((ka_count, rows, LANES), BF16),
            jax.ShapeDtypeStruct((2,), jnp.int32),
        )
        + tuple(jax.ShapeDtypeStruct(x.shape, x.dtype) for x in bring),
        in_specs=[smem, smem] + [hbm] * (1 + count),
        out_specs=(vmem, smem) + (vmem,) * count,
        scratch_shapes=[
            pltpu.VMEM(sketch.shape, BF16),
            pltpu.VMEM((ranks, rows, LANES), BF16),
            pltpu.SemaphoreType.DMA((count + 1,)),
        ],
        compiler_params=pltpu.CompilerParams(vmem_limit_bytes=8 << 20),
        name="pick_rows",
    )(told, me, *[pltpu.with_memory_space_constraint(x, pltpu.HBM) for x in (sketch, *bring)])


def keep_mask(facts, rows, cols):
    slot = iota((rows, 1), 0) >> 4
    top = jnp.where(slot < facts[1], facts[0] + slot + SLOTS // 2, -1)
    group = iota((1, cols), 1) >> 4
    return group.astype(F32).astype(BF16) <= top.astype(F32).astype(BF16)


def inverse_factor(work, offset, down=True):
    for batch in range(0, R, BATCH):
        order = [c if down else R - 1 - c for c in range(batch, batch + BATCH)]
        edge = (order[0] // 8) * 8
        low, high = (edge, R) if down else (0, edge + 8)
        part = work[low:high]
        rows = high - low
        place = low + iota((rows, LANES), 0)
        columns = [
            jnp.broadcast_to(part[:, offset + c : offset + c + 1], (rows, LANES)) for c in order
        ]
        for step, pivot in enumerate(order):
            at = pivot - low
            column = columns[step]
            scale = 1.0 / column[at : at + 1]
            rest = jnp.where(place > pivot if down else place < pivot, column, 0.0)
            for later in range(step + 1, BATCH):
                columns[later] = columns[later] - rest * (columns[later][at : at + 1] * scale)
            part = part - rest * (part[at : at + 1] * scale)
        pieces = [work[:low]] * (low > 0) + [part] + [work[high:]] * (high < R)
        work = pieces[0] if len(pieces) == 1 else jnp.concatenate(pieces, axis=0)
    lane, row = iota((R, LANES), 1), iota((R, LANES), 0)
    diag = jnp.sum(jnp.where(lane == row + offset, work, 0.0), axis=1, keepdims=True)
    return work * lax.rsqrt(diag)


def factor_pair(gram, last_up):
    left = iota((R, LANES), 1) < R
    eye = unit()
    first = inverse_factor(jnp.where(left, gram, eye), 0)
    second = inverse_factor(jnp.where(left, eye, gram), R, down=not last_up)
    turned = pltpu.roll(second, R, 1)
    zero = jnp.zeros((R, LANES), F32)
    inverse = jnp.concatenate(
        [jnp.where(left, pltpu.roll(first, R, 1), zero), jnp.where(left, zero, turned)], axis=0
    )
    return first, turned, inverse


def unit():
    lane, row = iota((R, LANES), 1), iota((R, LANES), 0)
    return jnp.where((lane & (R - 1)) == row, 1.0, 0.0).astype(F32)


def grams(both):
    square = dot(both, both, ((0,), (0,)), HIGH)
    return jnp.where(iota((R, LANES), 1) < R, square[:R], square[R:])


def three_terms(value):
    high = value.astype(BF16)
    rest = value - high.astype(F32)
    middle = rest.astype(BF16)
    return [high, middle, (rest - middle.astype(F32)).astype(BF16)]


def sketch_panels(facts, chosen, panel, sigma, basis, coef, copies):
    def kernel(facts, chosen, far, sigma, basis, coef, sketched, shared, panel, sem):
        k_count, rows, cols = panel.shape
        loads = [pltpu.make_async_copy(far.at[k], panel.at[k], sem.at[k]) for k in range(k_count)]
        for load in loads:
            load.start()
        row, col = iota((OO, OO), 0), iota((OO, OO), 1)
        inner = (row & 15) == (col >> 4)
        spread = jnp.where((row & 15) == (col & 15), 1.0, 0.0).astype(F32)
        same = (row >> 4) == (col >> 4)
        lines = []
        for k in range(k_count):
            summed = dot(basis[...], sigma[k], ((1,), (0,)))
            pairs = dot(summed, coef[k].astype(F32), ((0,), (0,)), HIGH)
            laid = dot(jnp.where(inner, pairs, 0.0), spread, ((1,), (0,)), HIGH)
            line = jnp.sum(jnp.where(same, laid, 0.0), axis=0, keepdims=True)
            lines += [line[:, :LANES], line[:, LANES:]]

        keep = keep_mask(facts, rows, cols)
        zero = jnp.zeros((rows, cols), BF16)
        parts = []
        for k in range(k_count):
            loads[k].wait()
            masked = jnp.where(keep, panel[k], zero)
            panel[k] = masked
            parts.append(dot(masked, chosen[...], ((1,), (0,))))
        both = jnp.where(iota((rows, LANES), 1) < R, parts[0], parts[1])
        sketched[...] = both

        gram = grams(both)
        lane, row = iota((R, LANES), 1), iota((R, LANES), 0)
        left = lane < R
        trace = jnp.sum(gram * unit(), axis=0, keepdims=True)
        half = lane[:1] < R
        shift = jnp.where(
            half,
            jnp.sum(jnp.where(half, trace, 0.0), axis=1, keepdims=True),
            jnp.sum(jnp.where(half, 0.0, trace), axis=1, keepdims=True),
        )
        shift = shift * (SHIFT / R) + TINY
        first, second, inverse = factor_pair(gram + unit() * shift, True)
        corners = jnp.where(lane >= row, first, second)
        folded = jnp.where(left[: R // 2], corners[: R // 2], pltpu.roll(corners, R, 1)[R // 2 :])
        diag = jnp.sum(jnp.where(lane == row, second, 0.0), axis=0, keepdims=True)
        told = [folded, diag, shift] + lines + [jnp.zeros((2, LANES), F32)]
        told = jnp.concatenate(three_terms(jnp.concatenate(told, axis=0)), axis=0)
        own = dot(inverse, both, ((1,), (1,)), HIGH).astype(BF16)
        chunk = cols // copies
        halves = chunk // LANES
        for place in range(copies):
            shared[place, k_count * halves * R :] = told
        for k in range(k_count):
            terms = dot(own, panel[k], ((1,), (0,)))[k * R : (k + 1) * R].astype(BF16)
            for place in range(copies):
                for part in range(halves):
                    at = place * chunk + part * LANES
                    base = (k * halves + part) * R
                    shared[place, base : base + R] = terms[:, at : at + LANES]

    k_count, rows, cols = panel.shape
    smem = pl.BlockSpec(memory_space=pltpu.SMEM)
    vmem = pl.BlockSpec(memory_space=pltpu.VMEM)
    hbm = pl.BlockSpec(memory_space=pltpu.HBM)
    told_rows = k_count * R * (cols // copies // LANES) + 3 * TOLD
    return pl.pallas_call(
        kernel,
        out_shape=(
            jax.ShapeDtypeStruct((rows, LANES), F32),
            jax.ShapeDtypeStruct((copies, told_rows, LANES), BF16),
        ),
        in_specs=[smem, vmem, hbm, vmem, vmem, vmem],
        out_specs=(vmem, vmem),
        scratch_shapes=[pltpu.VMEM(panel.shape, BF16), pltpu.SemaphoreType.DMA((k_count,))],
        compiler_params=pltpu.CompilerParams(vmem_limit_bytes=20 << 20),
        name="sketch_panels",
    )(facts, chosen, pltpu.with_memory_space_constraint(panel, pltpu.HBM), sigma, basis, coef)


def finish_panels(told, sketched, green, hamilton, chunk):
    def kernel(told, sketched, green, hamilton, next_green, ortho, right):
        k_count, copies = green.shape[0], told.shape[0]
        halves = chunk // LANES
        top = k_count * halves * R
        lane, row = iota((R, LANES), 1), iota((R, LANES), 0)
        left = lane < R
        factors, extra = [], jnp.zeros((TOLD - R // 2, LANES), F32)
        for place in range(copies):
            high, middle, low = (
                told[place, top + i * TOLD : top + (i + 1) * TOLD].astype(F32) for i in range(3)
            )
            value = high + middle + low
            extra = extra + value[R // 2 :]
            corners = value[: R // 2]
            turned = pltpu.roll(corners, R, 1)
            diag = pltpu.roll(value[R // 2 : R // 2 + 1], R, 1)
            upper = jnp.concatenate([corners, turned], axis=0)
            lower = jnp.concatenate([turned, corners], axis=0)
            lower = jnp.where(
                lane - R < row, lower, jnp.where(lane - R == row, diag, jnp.zeros_like(lower))
            )
            factors.append(jnp.where(left, jnp.where(lane >= row, upper, 0.0), lower))
        factors = jnp.concatenate(factors, axis=0)
        _, _, inverse = factor_pair(grams(factors) - unit() * extra[1:2], False)

        first = factors.astype(BF16)
        second = (factors - first.astype(F32)).astype(BF16)
        sums = []
        for k in range(k_count):
            terms = [
                jnp.concatenate(
                    [
                        told[place, (k * halves + part) * R : (k * halves + part + 1) * R]
                        for place in range(copies)
                    ],
                    axis=0,
                )
                for part in range(halves)
            ]
            terms = jnp.concatenate(terms, axis=1)
            both = dot(first, terms, ((0,), (0,))) + dot(second, terms, ((0,), (0,)))
            sums.append(both[k * R : (k + 1) * R])
        coeffs = dot(inverse, jnp.concatenate(sums, axis=0), ((1,), (0,)), HIGH)
        turned = dot(inverse, sketched[...], ((1,), (1,)), HIGH)
        for k in range(k_count):
            right[k] = coeffs[k * R : (k + 1) * R]
            ortho[k] = turned[k * R : (k + 1) * R]

        outer = (iota((NO, OO), 1) >> 4) == iota((NO, OO), 0)
        tile = jnp.where((iota((NO, OO), 1) & 15) == iota((NO, OO), 0), 1.0, 0.0).astype(F32)

        def square(line):
            return dot(jnp.where(outer, line, 0.0), tile, ((1,), (1,)), HIGH)

        for k in range(k_count):
            base = 2 + 2 * k
            line = jnp.concatenate([extra[base : base + 1], extra[base + 1 : base + 2]], axis=1)
            rate = square(line) * (1.0 / 256.0)
            g, h = square(green[k : k + 1]), square(hamilton[k : k + 1])
            for _ in range(2):
                left_prod = dot(h, g, ((1,), (0,)), HIGH)
                right_prod = dot(g, h, ((1,), (0,)), HIGH)
                g = g + STEP * (left_prod - right_prod + rate)
            flat = jnp.where(outer, dot(g, tile, ((1,), (0,)), HIGH), 0.0)
            next_green[k : k + 1] = jnp.sum(flat, axis=0, keepdims=True)

    k_count, rows = green.shape[0], sketched.shape[0]
    vmem = pl.BlockSpec(memory_space=pltpu.VMEM)
    return pl.pallas_call(
        kernel,
        out_shape=(
            jax.ShapeDtypeStruct((k_count, OO), F32),
            jax.ShapeDtypeStruct((k_count, R, rows), F32),
            jax.ShapeDtypeStruct((k_count, R, chunk), F32),
        ),
        in_specs=[vmem] * 4,
        out_specs=(vmem, vmem, vmem),
        compiler_params=pltpu.CompilerParams(vmem_limit_bytes=20 << 20),
        name="finish_panels",
    )(told, sketched, green, hamilton)


def body(
    sigma_history,
    time_basis,
    history_coef,
    green_now,
    hamilton,
    panel_block,
    panel_lengths,
    owners,
    sketch,
):
    ka_count, ta_count = lax.axis_size("ka"), lax.axis_size("ta")
    k_count = green_now.shape[0]
    assert NO * sigma_history.shape[1] * ta_count == 65536 and k_count == 2
    groups = [
        [place * ta_count + (group + place) % ta_count for place in range(ka_count)]
        for group in range(ta_count)
    ]
    facts = jnp.concatenate(
        [owners[:, 0], panel_lengths, lax.axis_index("ta").astype(jnp.int32).reshape(1)]
    )
    facts = jnp.pad(facts, (0, LANES - 4))
    told = lax.all_to_all(
        jnp.broadcast_to(facts[None, None], (ka_count, 1, LANES)),
        ("ka", "ta"),
        0,
        0,
        axis_index_groups=groups,
    ).reshape(ka_count, LANES)
    bring = (sigma_history, time_basis.T, history_coef)
    picked, facts, sigma, basis, coef = pick_rows(ka_count, ta_count, told, sketch, bring)
    chosen = lax.all_to_all(picked, "ka", 0, 0).reshape(-1, LANES)
    sketched, shared = sketch_panels(facts, chosen, panel_block, sigma, basis, coef, ta_count)
    told = lax.all_to_all(shared, "ta", 0, 0)
    chunk = panel_block.shape[2] // ta_count
    green_next, ortho, right = finish_panels(told, sketched, green_now, hamilton, chunk)
    return (green_next, ortho.transpose(0, 2, 1), right)


def solution(mesh):
    in_specs = (
        P("ka", "ta", None),
        P("ta", None),
        P("ka", "ta", None),
        P("ka", None),
        P("ka", None),
        P("ka", "ta", None),
        P("ta"),
        P("ka", None),
        P(None, "ka", None),
    )
    out_specs = (P("ka", None), P("ka", "ta", None), P("ka", None, "ta"))
    return jax.shard_map(body, mesh=mesh, in_specs=in_specs, out_specs=out_specs, check_vma=False)
```

```python
import jax
import jax.numpy as jnp
from jax import lax
from jax.experimental import pallas as pl
from jax.experimental.pallas import tpu as pltpu
from jax.sharding import PartitionSpec as P

NO = 16
OO = NO * NO
R = 64
SLOTS = 16
TOTAL = 120
LANES = 128
STEP = 0.25
BATCH = 8
TOLD = R // 2 + 8
SHIFT = 2.0**-12
TINY = 1e-30
HIGH = lax.Precision.HIGHEST
F32 = jnp.float32
BF16 = jnp.bfloat16


def turn(place):
    return ((place >> 1) & 1) | ((place >> 3) & 2)


def dot(left, right, contract, precision=None):
    return lax.dot_general(
        left, right, (contract, ((), ())), precision=precision, preferred_element_type=F32
    )


def iota(shape, dim):
    return lax.broadcasted_iota(jnp.int32, shape, dim)


def pick_rows(ka_count, ta_count, told, me, sketch, bring):
    count = len(bring)
    shapes = [x.shape for x in bring[:-1]] + [bring[-1].shape[1:]]

    def kernel(told, me, sketch_far, *refs):
        far, (picked, facts), near = refs[:count], refs[count : count + 2], refs[count + 2 :]
        near, (sketch, double, sem) = near[:count], near[count:]
        load = pltpu.make_async_copy(sketch_far, sketch, sem.at[count])
        load.start()
        loads = [
            pltpu.make_async_copy(
                far[i] if far[i].shape == near[i].shape else far[i].at[0], near[i], sem.at[i]
            )
            for i in range(count)
        ]
        for other in loads:
            other.start()
        before = jnp.int32(0)
        after = jnp.int32(0)
        length = jnp.int32(0)
        for place in (0, 2, 16, 18):
            where_from, amount = told[place, 3], told[place, 2]
            before = before + jnp.where(where_from < me[0], amount, 0)
            after = after + jnp.where(where_from >= me[0], amount, 0)
            length = length + jnp.where(where_from == me[0], amount, 0)
        facts[0] = jnp.where(me[0] < ta_count // 2, before, TOTAL - after)
        facts[1] = length
        load.wait()
        for rank in range(sketch.shape[0]):
            rows = sketch[rank]
            double[rank] = jnp.concatenate([rows, rows], axis=1)
        left = iota(double.shape[1:], 1) < R

        def one(place, carry):
            picked[place] = jnp.where(left, double[told[place, 0]], double[told[place, 1]])
            return carry

        lax.fori_loop(0, ka_count, one, 0, unroll=8)
        for other in loads:
            other.wait()

    ranks, rows, _ = sketch.shape
    smem = pl.BlockSpec(memory_space=pltpu.SMEM)
    vmem = pl.BlockSpec(memory_space=pltpu.VMEM)
    hbm = pl.BlockSpec(memory_space=pltpu.HBM)
    return pl.pallas_call(
        kernel,
        out_shape=(
            jax.ShapeDtypeStruct((ka_count, rows, LANES), BF16),
            jax.ShapeDtypeStruct((2,), jnp.int32),
        )
        + tuple(jax.ShapeDtypeStruct(shape, x.dtype) for x, shape in zip(bring, shapes)),
        in_specs=[smem] * 2 + [hbm] * (1 + count),
        out_specs=(vmem, smem) + (vmem,) * count,
        scratch_shapes=[
            pltpu.VMEM(sketch.shape, BF16),
            pltpu.VMEM((ranks, rows, LANES), BF16),
            pltpu.SemaphoreType.DMA((count + 1,)),
        ],
        compiler_params=pltpu.CompilerParams(vmem_limit_bytes=8 << 20),
        name="pick_rows",
    )(told, me, *[pltpu.with_memory_space_constraint(x, pltpu.HBM) for x in (sketch, *bring)])


def keep_mask(facts, rows, cols):
    slot = iota((rows, 1), 0) >> 4
    top = jnp.where(slot < facts[1], facts[0] + slot + SLOTS // 2, -1)
    group = iota((1, cols), 1) >> 4
    return group.astype(F32).astype(BF16) <= top.astype(F32).astype(BF16)


def inverse_factor(work, offset, down=True):
    for batch in range(0, R, BATCH):
        order = [c if down else R - 1 - c for c in range(batch, batch + BATCH)]
        edge = (order[0] // 8) * 8
        low, high = (edge, R) if down else (0, edge + 8)
        part = work[low:high]
        rows = high - low
        place = low + iota((rows, LANES), 0)
        columns = [
            jnp.broadcast_to(part[:, offset + c : offset + c + 1], (rows, LANES)) for c in order
        ]
        for step, pivot in enumerate(order):
            at = pivot - low
            column = columns[step]
            scale = 1.0 / column[at : at + 1]
            rest = jnp.where(place > pivot if down else place < pivot, column, 0.0)
            for later in range(step + 1, BATCH):
                columns[later] = columns[later] - rest * (columns[later][at : at + 1] * scale)
            part = part - rest * (part[at : at + 1] * scale)
        pieces = [work[:low]] * (low > 0) + [part] + [work[high:]] * (high < R)
        work = pieces[0] if len(pieces) == 1 else jnp.concatenate(pieces, axis=0)
    lane, row = iota((R, LANES), 1), iota((R, LANES), 0)
    diag = jnp.sum(jnp.where(lane == row + offset, work, 0.0), axis=1, keepdims=True)
    return work * lax.rsqrt(diag)


def factor_pair(gram, last_up):
    left = iota((R, LANES), 1) < R
    eye = unit()
    first = inverse_factor(jnp.where(left, gram, eye), 0)
    second = inverse_factor(jnp.where(left, eye, gram), R, down=not last_up)
    turned = pltpu.roll(second, R, 1)
    zero = jnp.zeros((R, LANES), F32)
    inverse = jnp.concatenate(
        [jnp.where(left, pltpu.roll(first, R, 1), zero), jnp.where(left, zero, turned)], axis=0
    )
    return first, turned, inverse


def split_dot(left, right, contract):
    (high, low), (top, rest) = (three_terms(x)[:2] for x in (left, right))
    return dot(
        jnp.concatenate([high, high, low], axis=contract[0][0]),
        jnp.concatenate([top, rest, top], axis=contract[1][0]),
        contract,
    )


def unit():
    lane, row = iota((R, LANES), 1), iota((R, LANES), 0)
    return jnp.where((lane & (R - 1)) == row, 1.0, 0.0).astype(F32)


def grams(both):
    square = dot(both, both, ((0,), (0,)), HIGH)
    return jnp.where(iota((R, LANES), 1) < R, square[:R], square[R:])


def three_terms(value):
    high = value.astype(BF16)
    rest = value - high.astype(F32)
    middle = rest.astype(BF16)
    return [high, middle, (rest - middle.astype(F32)).astype(BF16)]


def sketch_panels(facts, chosen, panel, first_panel, sigma, basis, coef, copies):
    def kernel(facts, chosen, far, near, sigma, basis, coef, sketched, shared, panel, sem):
        k_count, rows, cols = panel.shape
        loads = [pltpu.make_async_copy(far.at[k], panel.at[k], sem.at[k]) for k in range(1, k_count)]
        for load in loads:
            load.start()
        row, col = iota((OO, OO), 0), iota((OO, OO), 1)
        inner = (row & 15) == (col >> 4)
        spread = jnp.where((row & 15) == (col & 15), 1.0, 0.0).astype(BF16)
        same = iota((NO, OO), 0) == (iota((NO, OO), 1) >> 4)
        groups = []
        for k in range(k_count):
            summed = dot(basis[...], sigma[k], ((1,), (0,)))
            summed = jnp.concatenate(three_terms(summed), axis=0)
            pairs = dot(summed, jnp.concatenate([coef[k]] * 3, axis=0), ((0,), (0,)))
            pairs = jnp.where(inner, pairs, 0.0).reshape(NO, NO, OO)
            groups += three_terms(jnp.sum(pairs, axis=1))
        laid = dot(jnp.concatenate(groups, axis=0), spread, ((1,), (0,)))
        lines = []
        for k in range(k_count):
            base = 3 * NO * k
            total = laid[base : base + NO] + laid[base + NO : base + 2 * NO]
            total = total + laid[base + 2 * NO : base + 3 * NO]
            line = jnp.sum(jnp.where(same, total, 0.0), axis=0, keepdims=True)
            lines += [line[:, :LANES], line[:, LANES:]]

        keep = keep_mask(facts, rows, cols)
        zero = jnp.zeros((rows, cols), BF16)
        parts = []
        for k in range(k_count):
            if k > 0:
                loads[k - 1].wait()
            masked = jnp.where(keep, panel[k] if k > 0 else near[...], zero)
            panel[k] = masked
            parts.append(dot(masked, chosen[...], ((1,), (0,))))
        both = jnp.where(iota((rows, LANES), 1) < R, parts[0], parts[1])
        sketched[...] = both

        gram = grams(both)
        lane, row = iota((R, LANES), 1), iota((R, LANES), 0)
        left = lane < R
        trace = jnp.sum(gram * unit(), axis=0, keepdims=True)
        half = lane[:1] < R
        shift = jnp.where(
            half,
            jnp.sum(jnp.where(half, trace, 0.0), axis=1, keepdims=True),
            jnp.sum(jnp.where(half, 0.0, trace), axis=1, keepdims=True),
        )
        shift = shift * (SHIFT / R) + TINY
        first, second, inverse = factor_pair(gram + unit() * shift, True)
        corners = jnp.where(lane >= row, first, second)
        folded = jnp.where(left[: R // 2], corners[: R // 2], pltpu.roll(corners, R, 1)[R // 2 :])
        diag = jnp.sum(jnp.where(lane == row, second, 0.0), axis=0, keepdims=True)
        told = [folded, diag, shift] + lines + [jnp.zeros((2, LANES), F32)]
        told = three_terms(jnp.concatenate(told, axis=0))
        told = jnp.concatenate(told + [jnp.zeros((128 - 3 * TOLD, LANES), BF16)], axis=0)
        own = split_dot(inverse, both, ((1,), (1,))).astype(BF16)
        chunk = cols // copies
        halves = chunk // LANES
        for place in range(copies):
            shared[place, k_count * halves * R :] = told
        for k in range(k_count):
            terms = dot(own, panel[k], ((1,), (0,)))[k * R : (k + 1) * R].astype(BF16)
            for place in range(copies):
                for part in range(halves):
                    at = place * chunk + part * LANES
                    base = (k * halves + part) * R
                    shared[place, base : base + R] = terms[:, at : at + LANES]

    k_count, rows, cols = panel.shape
    smem = pl.BlockSpec(memory_space=pltpu.SMEM)
    vmem = pl.BlockSpec(memory_space=pltpu.VMEM)
    hbm = pl.BlockSpec(memory_space=pltpu.HBM)
    told_rows = k_count * R * (cols // copies // LANES) + 128
    return pl.pallas_call(
        kernel,
        out_shape=(
            jax.ShapeDtypeStruct((rows, LANES), F32),
            jax.ShapeDtypeStruct((copies, told_rows, LANES), BF16),
        ),
        in_specs=[smem, vmem, hbm, vmem, vmem, vmem, vmem],
        out_specs=(vmem, vmem),
        scratch_shapes=[pltpu.VMEM(panel.shape, BF16), pltpu.SemaphoreType.DMA((k_count,))],
        compiler_params=pltpu.CompilerParams(vmem_limit_bytes=20 << 20),
        name="sketch_panels",
    )(
        facts,
        chosen,
        pltpu.with_memory_space_constraint(panel, pltpu.HBM),
        first_panel,
        sigma,
        basis,
        coef,
    )


def finish_panels(told, sketched, green, hamilton, chunk):
    def kernel(told, sketched, green, hamilton, next_green, ortho, right):
        k_count, copies = green.shape[0], told.shape[0]
        halves = chunk // LANES
        top = k_count * halves * R
        lane, row = iota((R, LANES), 1), iota((R, LANES), 0)
        left = lane < R
        factors, extra = [], jnp.zeros((TOLD - R // 2, LANES), F32)
        for place in range(copies):
            high, middle, low = (
                told[place, top + i * TOLD : top + (i + 1) * TOLD].astype(F32) for i in range(3)
            )
            value = high + middle + low
            extra = extra + value[R // 2 :]
            corners = value[: R // 2]
            turned = pltpu.roll(corners, R, 1)
            diag = pltpu.roll(value[R // 2 : R // 2 + 1], R, 1)
            upper = jnp.concatenate([corners, turned], axis=0)
            lower = jnp.concatenate([turned, corners], axis=0)
            lower = jnp.where(
                lane - R < row, lower, jnp.where(lane - R == row, diag, jnp.zeros_like(lower))
            )
            factors.append(jnp.where(left, jnp.where(lane >= row, upper, 0.0), lower))
        outer = (iota((NO, OO), 1) >> 4) == iota((NO, OO), 0)
        tile = jnp.where((iota((NO, OO), 1) & 15) == iota((NO, OO), 0), 1.0, 0.0).astype(F32)

        def square(line):
            return dot(jnp.where(outer, line, 0.0), tile, ((1,), (1,)), HIGH)

        for k in range(k_count):
            base = 2 + 2 * k
            line = jnp.concatenate([extra[base : base + 1], extra[base + 1 : base + 2]], axis=1)
            rate = square(line) * (1.0 / 256.0)
            g, h = square(green[k : k + 1]), square(hamilton[k : k + 1])
            for _ in range(2):
                left_prod = dot(h, g, ((1,), (0,)), HIGH)
                right_prod = dot(g, h, ((1,), (0,)), HIGH)
                g = g + STEP * (left_prod - right_prod + rate)
            flat = jnp.where(outer, dot(g, tile, ((1,), (0,)), HIGH), 0.0)
            next_green[k : k + 1] = jnp.sum(flat, axis=0, keepdims=True)

        factors = jnp.concatenate(factors, axis=0)
        _, _, inverse = factor_pair(grams(factors) - unit() * extra[1:2], False)

        first = factors.astype(BF16)
        second = (factors - first.astype(F32)).astype(BF16)
        sums = []
        for k in range(k_count):
            terms = [
                jnp.concatenate(
                    [
                        told[place, (k * halves + part) * R : (k * halves + part + 1) * R]
                        for place in range(copies)
                    ],
                    axis=0,
                )
                for part in range(halves)
            ]
            terms = jnp.concatenate(terms, axis=1)
            both = dot(first, terms, ((0,), (0,))) + dot(second, terms, ((0,), (0,)))
            sums.append(both[k * R : (k + 1) * R])
        coeffs = split_dot(inverse, jnp.concatenate(sums, axis=0), ((1,), (0,)))
        turned = split_dot(inverse, sketched[...], ((1,), (1,)))
        for k in range(k_count):
            right[k] = coeffs[k * R : (k + 1) * R]
            ortho[k] = turned[k * R : (k + 1) * R]

    k_count, rows = green.shape[0], sketched.shape[0]
    vmem = pl.BlockSpec(memory_space=pltpu.VMEM)
    return pl.pallas_call(
        kernel,
        out_shape=(
            jax.ShapeDtypeStruct((k_count, OO), F32),
            jax.ShapeDtypeStruct((k_count, R, rows), F32),
            jax.ShapeDtypeStruct((k_count, R, chunk), F32),
        ),
        in_specs=[vmem] * 4,
        out_specs=(vmem, vmem, vmem),
        compiler_params=pltpu.CompilerParams(vmem_limit_bytes=20 << 20),
        name="finish_panels",
    )(told, sketched, green, hamilton)


def body(
    sigma_history,
    time_basis,
    history_coef,
    green_now,
    hamilton,
    panel_block,
    panel_lengths,
    owners,
    sketch,
):
    ka_count, ta_count = lax.axis_size("ka"), lax.axis_size("ta")
    k_count = green_now.shape[0]
    assert NO * sigma_history.shape[1] * ta_count == 65536 and k_count == 2
    groups = [
        [place * ta_count + (group ^ turn(place)) for place in range(ka_count)]
        for group in range(ta_count)
    ]
    me = lax.axis_index("ta").astype(jnp.int32).reshape(1)
    asked = jnp.pad(owners.reshape(1, 2), ((0, 0), (0, LANES - 2)))
    asked = asked + jnp.pad(panel_lengths[None], ((0, 0), (2, LANES - 3)))
    asked = asked + jnp.where(iota((1, LANES), 1) == 3, me[0], 0)
    asked = jnp.broadcast_to(asked[None], (ka_count, 1, LANES))
    told = lax.all_to_all(
        asked,
        ("ka", "ta"),
        0,
        0,
        axis_index_groups=groups,
    ).reshape(ka_count, LANES)
    bring = (sigma_history, time_basis.T, history_coef, panel_block)
    picked, facts, sigma, basis, coef, panel = pick_rows(
        ka_count, ta_count, told, me, sketch, bring
    )
    chosen = lax.all_to_all(picked, "ka", 0, 0).reshape(-1, LANES)
    sketched, shared = sketch_panels(
        facts, chosen, panel_block, panel, sigma, basis, coef, ta_count
    )
    told = lax.all_to_all(shared, "ta", 0, 0)
    chunk = panel_block.shape[2] // ta_count
    green_next, ortho, right = finish_panels(told, sketched, green_now, hamilton, chunk)
    return (green_next, ortho.transpose(0, 2, 1), right)


def solution(mesh):
    in_specs = (
        P("ka", "ta", None),
        P("ta", None),
        P("ka", "ta", None),
        P("ka", None),
        P("ka", None),
        P("ka", "ta", None),
        P("ta"),
        P("ka", None),
        P(None, "ka", None),
    )
    out_specs = (P("ka", None), P("ka", "ta", None), P("ka", None, "ta"))
    return jax.shard_map(body, mesh=mesh, in_specs=in_specs, out_specs=out_specs, check_vma=False)
```

```python
import jax
import jax.numpy as jnp
from jax import lax
from jax.experimental import pallas as pl
from jax.experimental.pallas import tpu as pltpu
from jax.sharding import PartitionSpec as P

NO = 16
OO = NO * NO
R = 64
SLOTS = 16
TOTAL = 120
LANES = 128
STEP = 0.25
BATCH = 8
TOLD = R // 2 + 8
SHIFT = 2.0**-12
TINY = 1e-30
HIGH = lax.Precision.HIGHEST
F32 = jnp.float32
BF16 = jnp.bfloat16


def turn(place):
    return ((place >> 1) & 1) | ((place >> 3) & 2)


def dot(left, right, contract, precision=None):
    return lax.dot_general(
        left, right, (contract, ((), ())), precision=precision, preferred_element_type=F32
    )


def iota(shape, dim):
    return lax.broadcasted_iota(jnp.int32, shape, dim)


def pick_rows(ka_count, ta_count, told, me, sketch, bring):
    count = len(bring)

    def kernel(told, me, sketch_far, *refs):
        far, (picked, facts), near = refs[:count], refs[count : count + 2], refs[count + 2 :]
        near, (sketch, double, sem) = near[:count], near[count:]
        load = pltpu.make_async_copy(sketch_far, sketch, sem.at[count])
        load.start()
        loads = [pltpu.make_async_copy(far[i], near[i], sem.at[i]) for i in range(count)]
        for other in loads:
            other.start()
        before = jnp.int32(0)
        after = jnp.int32(0)
        length = jnp.int32(0)
        for place in (0, 2, 16, 18):
            where_from, amount = told[place, 3], told[place, 2]
            before = before + jnp.where(where_from < me[0], amount, 0)
            after = after + jnp.where(where_from >= me[0], amount, 0)
            length = length + jnp.where(where_from == me[0], amount, 0)
        facts[0] = jnp.where(me[0] < ta_count // 2, before, TOTAL - after)
        facts[1] = length
        load.wait()
        for rank in range(sketch.shape[0]):
            rows = sketch[rank]
            double[rank] = jnp.concatenate([rows, rows], axis=1)
        left = iota(double.shape[1:], 1) < R

        def one(place, carry):
            picked[place] = jnp.where(left, double[told[place, 0]], double[told[place, 1]])
            return carry

        lax.fori_loop(0, ka_count, one, 0, unroll=8)
        for other in loads:
            other.wait()

    ranks, rows, _ = sketch.shape
    smem = pl.BlockSpec(memory_space=pltpu.SMEM)
    vmem = pl.BlockSpec(memory_space=pltpu.VMEM)
    hbm = pl.BlockSpec(memory_space=pltpu.HBM)
    return pl.pallas_call(
        kernel,
        out_shape=(
            jax.ShapeDtypeStruct((ka_count, rows, LANES), BF16),
            jax.ShapeDtypeStruct((2,), jnp.int32),
        )
        + tuple(jax.ShapeDtypeStruct(x.shape, x.dtype) for x in bring),
        in_specs=[smem] * 2 + [hbm] * (1 + count),
        out_specs=(vmem, smem) + (vmem,) * count,
        scratch_shapes=[
            pltpu.VMEM(sketch.shape, BF16),
            pltpu.VMEM((ranks, rows, LANES), BF16),
            pltpu.SemaphoreType.DMA((count + 1,)),
        ],
        compiler_params=pltpu.CompilerParams(vmem_limit_bytes=8 << 20),
        name="pick_rows",
    )(told, me, *[pltpu.with_memory_space_constraint(x, pltpu.HBM) for x in (sketch, *bring)])


def keep_mask(facts, rows, cols):
    slot = iota((rows, 1), 0) >> 4
    top = jnp.where(slot < facts[1], facts[0] + slot + SLOTS // 2, -1)
    group = iota((1, cols), 1) >> 4
    return group.astype(F32).astype(BF16) <= top.astype(F32).astype(BF16)


def together(*stages):
    results, running = {}, dict(enumerate(stages))
    while running:
        for place, stage in list(running.items()):
            try:
                next(stage)
            except StopIteration as end:
                results[place] = end.value
                del running[place]
    return [results[place] for place in range(len(stages))]


def inverse_factor(work, offset, down=True):
    for batch in range(0, R, BATCH):
        order = [c if down else R - 1 - c for c in range(batch, batch + BATCH)]
        edge = (order[0] // 8) * 8
        low, high = (edge, R) if down else (0, edge + 8)
        part = work[low:high]
        rows = high - low
        place = low + iota((rows, LANES), 0)
        columns = [
            jnp.broadcast_to(part[:, offset + c : offset + c + 1], (rows, LANES)) for c in order
        ]
        for step, pivot in enumerate(order):
            at = pivot - low
            column = columns[step]
            scale = 1.0 / column[at : at + 1]
            rest = jnp.where(place > pivot if down else place < pivot, column, 0.0)
            for later in range(step + 1, BATCH):
                columns[later] = columns[later] - rest * (columns[later][at : at + 1] * scale)
            part = part - rest * (part[at : at + 1] * scale)
        pieces = [work[:low]] * (low > 0) + [part] + [work[high:]] * (high < R)
        work = pieces[0] if len(pieces) == 1 else jnp.concatenate(pieces, axis=0)
        yield
    lane, row = iota((R, LANES), 1), iota((R, LANES), 0)
    diag = jnp.sum(jnp.where(lane == row + offset, work, 0.0), axis=1, keepdims=True)
    return work * lax.rsqrt(diag)


def inverse_pair(work):
    width = 8
    spot = iota((R, LANES), 1) & (R - 1)
    row, left = iota((R, LANES), 0), iota((R, LANES), 1) < R
    one, own_row = spot[:1], row[:width]
    for start in range(0, R, width):
        top, rest = work[start : start + width], work[start + width :]
        part = work[start:]
        columns = [
            jnp.where(
                left[start:],
                jnp.broadcast_to(part[:, c : c + 1], part.shape),
                jnp.broadcast_to(part[:, R + c : R + c + 1], part.shape),
            )
            for c in range(start, start + width)
        ]
        inside = (one >= start) & (one < start + width)
        rest = jnp.where(inside, 0.0, rest)
        for step in range(width):
            pivot = start + step
            column = columns[step]
            scale = 1.0 / column[step : step + 1]
            upper = jnp.where(own_row > step, column[:width], 0.0)
            column = jnp.concatenate([upper, column[width:]], axis=0) if start + width < R else upper
            for later in range(step + 1, width):
                columns[later] = columns[later] - column * (columns[later][step : step + 1] * scale)
            line = jnp.where(one == pivot, 1.0, top[step : step + 1]) * scale
            gone = (spot[:width] == pivot) & (own_row > step)
            top = jnp.where(gone, 0.0, top) - upper * line
            if start + width < R:
                rest = rest - column[width:] * jnp.where(inside & (one > pivot), 0.0, line)
        pieces = [work[:start]] * (start > 0) + [top] + [rest] * (start + width < R)
        work = jnp.concatenate(pieces, axis=0)
        yield
    diag = jnp.where(spot == row, work, 0.0)
    scale = jnp.where(
        left,
        lax.rsqrt(jnp.sum(jnp.where(left, diag, 0.0), axis=1, keepdims=True)),
        lax.rsqrt(jnp.sum(jnp.where(left, 0.0, diag), axis=1, keepdims=True)),
    )
    work = jnp.where(spot < row, work * scale, jnp.where(spot == row, scale, 0.0))
    return jnp.concatenate([jnp.where(left, work, 0.0), jnp.where(left, 0.0, work)], axis=0)


def factor_pair(gram, beside):
    left = iota((R, LANES), 1) < R
    eye = unit()
    first, second, other = together(
        inverse_factor(jnp.where(left, gram, eye), 0),
        inverse_factor(jnp.where(left, eye, gram), R, down=False),
        beside,
    )
    turned = pltpu.roll(second, R, 1)
    zero = jnp.zeros((R, LANES), F32)
    inverse = jnp.concatenate(
        [jnp.where(left, pltpu.roll(first, R, 1), zero), jnp.where(left, zero, turned)], axis=0
    )
    return first, turned, inverse, other


def split_dot(left, right, contract):
    (high, low), (top, rest) = (three_terms(x)[:2] for x in (left, right))
    return dot(
        jnp.concatenate([high, high, low], axis=contract[0][0]),
        jnp.concatenate([top, rest, top], axis=contract[1][0]),
        contract,
    )


def unit():
    lane, row = iota((R, LANES), 1), iota((R, LANES), 0)
    return jnp.where((lane & (R - 1)) == row, 1.0, 0.0).astype(F32)


def grams(both):
    square = dot(both, both, ((0,), (0,)), HIGH)
    return jnp.where(iota((R, LANES), 1) < R, square[:R], square[R:])


def three_terms(value):
    high = value.astype(BF16)
    rest = value - high.astype(F32)
    middle = rest.astype(BF16)
    return [high, middle, (rest - middle.astype(F32)).astype(BF16)]


def sketch_panels(facts, chosen, panel, sigma, basis, coef, copies):
    def kernel(facts, chosen, near, sigma, basis, coef, sketched, shared, panel):
        k_count, rows, cols = panel.shape

        def history():
            row, col = iota((OO, OO), 0), iota((OO, OO), 1)
            inner = (row & 15) == (col >> 4)
            spread = jnp.where((row & 15) == (col & 15), 1.0, 0.0).astype(BF16)
            same = iota((NO, OO), 0) == (iota((NO, OO), 1) >> 4)
            groups = []
            for k in range(k_count):
                summed = dot(basis[...], sigma[k], ((1,), (0,)))
                yield
                summed = jnp.concatenate(three_terms(summed), axis=0)
                pairs = dot(summed, jnp.concatenate([coef[k]] * 3, axis=0), ((0,), (0,)))
                yield
                pairs = jnp.where(inner, pairs, 0.0).reshape(NO, NO, OO)
                groups += three_terms(jnp.sum(pairs, axis=1))
                yield
            laid = dot(jnp.concatenate(groups, axis=0), spread, ((1,), (0,)))
            yield
            lines = []
            for k in range(k_count):
                base = 3 * NO * k
                total = laid[base : base + NO] + laid[base + NO : base + 2 * NO]
                total = total + laid[base + 2 * NO : base + 3 * NO]
                line = jnp.sum(jnp.where(same, total, 0.0), axis=0, keepdims=True)
                lines += [line[:, :LANES], line[:, LANES:]]
            return lines

        keep = keep_mask(facts, rows, cols)
        zero = jnp.zeros((rows, cols), BF16)
        parts = []
        for k in range(k_count):
            masked = jnp.where(keep, near[k], zero)
            panel[k] = masked
            parts.append(dot(masked, chosen[...], ((1,), (0,))))
        both = jnp.where(iota((rows, LANES), 1) < R, parts[0], parts[1])
        sketched[...] = both

        gram = grams(both)
        lane, row = iota((R, LANES), 1), iota((R, LANES), 0)
        left = lane < R
        trace = jnp.sum(gram * unit(), axis=0, keepdims=True)
        half = lane[:1] < R
        shift = jnp.where(
            half,
            jnp.sum(jnp.where(half, trace, 0.0), axis=1, keepdims=True),
            jnp.sum(jnp.where(half, 0.0, trace), axis=1, keepdims=True),
        )
        shift = shift * (SHIFT / R) + TINY
        first, second, inverse, lines = factor_pair(gram + unit() * shift, history())
        corners = jnp.where(lane >= row, first, second)
        folded = jnp.where(left[: R // 2], corners[: R // 2], pltpu.roll(corners, R, 1)[R // 2 :])
        diag = jnp.sum(jnp.where(lane == row, second, 0.0), axis=0, keepdims=True)
        told = [folded, diag, shift] + lines + [jnp.zeros((2, LANES), F32)]
        told = three_terms(jnp.concatenate(told, axis=0))
        told = jnp.concatenate(told + [jnp.zeros((128 - 3 * TOLD, LANES), BF16)], axis=0)
        own = split_dot(inverse, both, ((1,), (1,))).astype(BF16)
        chunk = cols // copies
        halves = chunk // LANES
        for place in range(copies):
            shared[place, k_count * halves * R :] = told
        for k in range(k_count):
            terms = dot(own, panel[k], ((1,), (0,)))[k * R : (k + 1) * R].astype(BF16)
            for place in range(copies):
                for part in range(halves):
                    at = place * chunk + part * LANES
                    base = (k * halves + part) * R
                    shared[place, base : base + R] = terms[:, at : at + LANES]

    k_count, rows, cols = panel.shape
    smem = pl.BlockSpec(memory_space=pltpu.SMEM)
    vmem = pl.BlockSpec(memory_space=pltpu.VMEM)
    told_rows = k_count * R * (cols // copies // LANES) + 128
    return pl.pallas_call(
        kernel,
        out_shape=(
            jax.ShapeDtypeStruct((rows, LANES), F32),
            jax.ShapeDtypeStruct((copies, told_rows, LANES), BF16),
        ),
        in_specs=[smem] + [vmem] * 5,
        out_specs=(vmem, vmem),
        scratch_shapes=[pltpu.VMEM(panel.shape, BF16)],
        compiler_params=pltpu.CompilerParams(vmem_limit_bytes=20 << 20),
        name="sketch_panels",
    )(facts, chosen, panel, sigma, basis, coef)


def finish_panels(told, sketched, green, hamilton, chunk):
    def kernel(told, sketched, green, hamilton, next_green, ortho, right):
        k_count, copies = green.shape[0], told.shape[0]
        halves = chunk // LANES
        top = k_count * halves * R
        lane, row = iota((R, LANES), 1), iota((R, LANES), 0)
        left = lane < R
        factors, extra = [], jnp.zeros((TOLD - R // 2, LANES), F32)
        for place in range(copies):
            high, middle, low = (
                told[place, top + i * TOLD : top + (i + 1) * TOLD].astype(F32) for i in range(3)
            )
            value = high + middle + low
            extra = extra + value[R // 2 :]
            corners = value[: R // 2]
            turned = pltpu.roll(corners, R, 1)
            diag = pltpu.roll(value[R // 2 : R // 2 + 1], R, 1)
            upper = jnp.concatenate([corners, turned], axis=0)
            lower = jnp.concatenate([turned, corners], axis=0)
            lower = jnp.where(
                lane - R < row, lower, jnp.where(lane - R == row, diag, jnp.zeros_like(lower))
            )
            factors.append(jnp.where(left, jnp.where(lane >= row, upper, 0.0), lower))
        factors = jnp.concatenate(factors, axis=0)

        def beside():
            outer = (iota((NO, OO), 1) >> 4) == iota((NO, OO), 0)
            tile = jnp.where((iota((NO, OO), 1) & 15) == iota((NO, OO), 0), 1.0, 0.0).astype(F32)

            def square(line):
                return dot(jnp.where(outer, line, 0.0), tile, ((1,), (1,)), HIGH)

            rates = []
            for k in range(k_count):
                base = 2 + 2 * k
                line = jnp.concatenate([extra[base : base + 1], extra[base + 1 : base + 2]], axis=1)
                rates.append(square(line) * (1.0 / 256.0))
            states = [square(green[k : k + 1]) for k in range(k_count)]
            operators = [square(hamilton[k : k + 1]) for k in range(k_count)]
            yield
            for _ in range(2):
                pairs = [
                    (dot(h, g, ((1,), (0,)), HIGH), dot(g, h, ((1,), (0,)), HIGH))
                    for g, h in zip(states, operators)
                ]
                states = [
                    g + STEP * (left_prod - right_prod + rate)
                    for g, (left_prod, right_prod), rate in zip(states, pairs, rates)
                ]
                yield
            for k in range(k_count):
                flat = jnp.where(outer, dot(states[k], tile, ((1,), (0,)), HIGH), 0.0)
                next_green[k : k + 1] = jnp.sum(flat, axis=0, keepdims=True)
            yield
            first = factors.astype(BF16)
            second = (factors - first.astype(F32)).astype(BF16)
            sums = []
            for k in range(k_count):
                terms = [
                    jnp.concatenate(
                        [
                            told[place, (k * halves + part) * R : (k * halves + part + 1) * R]
                            for place in range(copies)
                        ],
                        axis=0,
                    )
                    for part in range(halves)
                ]
                terms = jnp.concatenate(terms, axis=1)
                both = dot(first, terms, ((0,), (0,))) + dot(second, terms, ((0,), (0,)))
                sums.append(both[k * R : (k + 1) * R])
                yield
            return jnp.concatenate(sums, axis=0)

        inverse, sums = together(
            inverse_pair(grams(factors) - unit() * extra[1:2]), beside()
        )
        coeffs = split_dot(inverse, sums, ((1,), (0,)))
        turned = split_dot(inverse, sketched[...], ((1,), (1,)))
        for k in range(k_count):
            right[k] = coeffs[k * R : (k + 1) * R]
            ortho[k] = turned[k * R : (k + 1) * R]

    k_count, rows = green.shape[0], sketched.shape[0]
    vmem = pl.BlockSpec(memory_space=pltpu.VMEM)
    return pl.pallas_call(
        kernel,
        out_shape=(
            jax.ShapeDtypeStruct((k_count, OO), F32),
            jax.ShapeDtypeStruct((k_count, R, rows), F32),
            jax.ShapeDtypeStruct((k_count, R, chunk), F32),
        ),
        in_specs=[vmem] * 4,
        out_specs=(vmem, vmem, vmem),
        compiler_params=pltpu.CompilerParams(vmem_limit_bytes=20 << 20),
        name="finish_panels",
    )(told, sketched, green, hamilton)


def body(
    sigma_history,
    time_basis,
    history_coef,
    green_now,
    hamilton,
    panel_block,
    panel_lengths,
    owners,
    sketch,
):
    ka_count, ta_count = lax.axis_size("ka"), lax.axis_size("ta")
    k_count = green_now.shape[0]
    assert NO * sigma_history.shape[1] * ta_count == 65536 and k_count == 2
    groups = [
        [place * ta_count + (group ^ turn(place)) for place in range(ka_count)]
        for group in range(ta_count)
    ]
    me = lax.axis_index("ta").astype(jnp.int32).reshape(1)
    asked = jnp.pad(owners.reshape(2), (0, LANES - 2)) + jnp.pad(panel_lengths, (2, LANES - 3))
    asked = asked + jnp.where(iota((1, LANES), 1)[0] == 3, me[0], 0)
    asked = jnp.broadcast_to(asked[None, None], (ka_count, 1, LANES))
    told = lax.all_to_all(
        asked,
        ("ka", "ta"),
        0,
        0,
        axis_index_groups=groups,
    ).reshape(ka_count, LANES)
    bring = (sigma_history, time_basis.T, history_coef, panel_block)
    picked, facts, sigma, basis, coef, panel = pick_rows(
        ka_count, ta_count, told, me, sketch, bring
    )
    chosen = lax.all_to_all(picked, "ka", 0, 0).reshape(-1, LANES)
    sketched, shared = sketch_panels(facts, chosen, panel, sigma, basis, coef, ta_count)
    told = lax.all_to_all(shared, "ta", 0, 0)
    chunk = panel_block.shape[2] // ta_count
    green_next, ortho, right = finish_panels(told, sketched, green_now, hamilton, chunk)
    return (green_next, ortho.transpose(0, 2, 1), right)


def solution(mesh):
    in_specs = (
        P("ka", "ta", None),
        P("ta", None),
        P("ka", "ta", None),
        P("ka", None),
        P("ka", None),
        P("ka", "ta", None),
        P("ta"),
        P("ka", None),
        P(None, "ka", None),
    )
    out_specs = (P("ka", None), P("ka", "ta", None), P("ka", None, "ta"))
    return jax.shard_map(body, mesh=mesh, in_specs=in_specs, out_specs=out_specs, check_vma=False)
```

```python
import jax
import jax.numpy as jnp
from jax import lax
from jax.experimental import pallas as pl
from jax.experimental.pallas import tpu as pltpu
from jax.sharding import PartitionSpec as P

NO = 16
OO = NO * NO
R = 64
SLOTS = 16
TOTAL = 120
LANES = 128
STEP = 0.25
BATCH = 8
TOLD = R // 2 + 8
SHIFT = 2.0**-12
TINY = 1e-30
HIGH = lax.Precision.HIGHEST
F32 = jnp.float32
BF16 = jnp.bfloat16


def turn(place):
    return place if place < 4 else 0


def dot(left, right, contract, precision=None):
    return lax.dot_general(
        left, right, (contract, ((), ())), precision=precision, preferred_element_type=F32
    )


def iota(shape, dim):
    return lax.broadcasted_iota(jnp.int32, shape, dim)


def pick_rows(ka_count, ta_count, told, me, sketch, bring):
    count = len(bring)

    def kernel(told, me, sketch_far, *refs):
        far, (picked, facts), near = refs[:count], refs[count : count + 2], refs[count + 2 :]
        near, (sketch, double, sem) = near[:count], near[count:]
        load = pltpu.make_async_copy(sketch_far, sketch, sem.at[count])
        load.start()
        loads = [pltpu.make_async_copy(far[i], near[i], sem.at[i]) for i in range(count)]
        for other in loads:
            other.start()
        before = jnp.int32(0)
        after = jnp.int32(0)
        length = jnp.int32(0)
        for place in range(4):
            where_from, amount = told[place, 3], told[place, 2]
            before = before + jnp.where(where_from < me[0], amount, 0)
            after = after + jnp.where(where_from >= me[0], amount, 0)
            length = length + jnp.where(where_from == me[0], amount, 0)
        facts[0] = jnp.where(me[0] < ta_count // 2, before, TOTAL - after)
        facts[1] = length
        load.wait()
        for rank in range(sketch.shape[0]):
            rows = sketch[rank]
            double[rank] = jnp.concatenate([rows, rows], axis=1)
        left = iota(double.shape[1:], 1) < R

        def one(place, carry):
            picked[place] = jnp.where(left, double[told[place, 0]], double[told[place, 1]])
            return carry

        lax.fori_loop(0, ka_count, one, 0, unroll=8)
        for other in loads:
            other.wait()

    ranks, rows, _ = sketch.shape
    smem = pl.BlockSpec(memory_space=pltpu.SMEM)
    vmem = pl.BlockSpec(memory_space=pltpu.VMEM)
    hbm = pl.BlockSpec(memory_space=pltpu.HBM)
    return pl.pallas_call(
        kernel,
        out_shape=(
            jax.ShapeDtypeStruct((ka_count, rows, LANES), BF16),
            jax.ShapeDtypeStruct((2,), jnp.int32),
        )
        + tuple(jax.ShapeDtypeStruct(x.shape, x.dtype) for x in bring),
        in_specs=[smem] * 2 + [hbm] * (1 + count),
        out_specs=(vmem, smem) + (vmem,) * count,
        scratch_shapes=[
            pltpu.VMEM(sketch.shape, BF16),
            pltpu.VMEM((ranks, rows, LANES), BF16),
            pltpu.SemaphoreType.DMA((count + 1,)),
        ],
        compiler_params=pltpu.CompilerParams(vmem_limit_bytes=8 << 20),
        name="pick_rows",
    )(told, me, *[pltpu.with_memory_space_constraint(x, pltpu.HBM) for x in (sketch, *bring)])


def keep_mask(facts, rows, cols):
    slot = iota((rows, 1), 0) >> 4
    top = jnp.where(slot < facts[1], facts[0] + slot + SLOTS // 2, -1)
    group = iota((1, cols), 1) >> 4
    return group.astype(F32).astype(BF16) <= top.astype(F32).astype(BF16)


def together(*stages):
    results, running = {}, dict(enumerate(stages))
    while running:
        for place, stage in list(running.items()):
            try:
                next(stage)
            except StopIteration as end:
                results[place] = end.value
                del running[place]
    return [results[place] for place in range(len(stages))]


def inverse_factor(work, offset, down=True):
    for batch in range(0, R, BATCH):
        order = [c if down else R - 1 - c for c in range(batch, batch + BATCH)]
        edge = (order[0] // 8) * 8
        low, high = (edge, R) if down else (0, edge + 8)
        part = work[low:high]
        rows = high - low
        place = low + iota((rows, LANES), 0)
        columns = [
            jnp.broadcast_to(part[:, offset + c : offset + c + 1], (rows, LANES)) for c in order
        ]
        for step, pivot in enumerate(order):
            at = pivot - low
            column = columns[step]
            scale = 1.0 / column[at : at + 1]
            rest = jnp.where(place > pivot if down else place < pivot, column, 0.0)
            for later in range(step + 1, BATCH):
                columns[later] = columns[later] - rest * (columns[later][at : at + 1] * scale)
            part = part - rest * (part[at : at + 1] * scale)
        pieces = [work[:low]] * (low > 0) + [part] + [work[high:]] * (high < R)
        work = pieces[0] if len(pieces) == 1 else jnp.concatenate(pieces, axis=0)
        yield
    lane, row = iota((R, LANES), 1), iota((R, LANES), 0)
    diag = jnp.sum(jnp.where(lane == row + offset, work, 0.0), axis=1, keepdims=True)
    return work * lax.rsqrt(diag)


def inverse_pair(work):
    width = 8
    spot = iota((R, LANES), 1) & (R - 1)
    row, left = iota((R, LANES), 0), iota((R, LANES), 1) < R
    one, own_row = spot[:1], row[:width]
    for start in range(0, R, width):
        top, rest = work[start : start + width], work[start + width :]
        part = work[start:]
        columns = [
            jnp.where(
                left[start:],
                jnp.broadcast_to(part[:, c : c + 1], part.shape),
                jnp.broadcast_to(part[:, R + c : R + c + 1], part.shape),
            )
            for c in range(start, start + width)
        ]
        inside = (one >= start) & (one < start + width)
        rest = jnp.where(inside, 0.0, rest)
        for step in range(width):
            pivot = start + step
            column = columns[step]
            scale = 1.0 / column[step : step + 1]
            upper = jnp.where(own_row > step, column[:width], 0.0)
            column = jnp.concatenate([upper, column[width:]], axis=0) if start + width < R else upper
            for later in range(step + 1, width):
                columns[later] = columns[later] - column * (columns[later][step : step + 1] * scale)
            line = jnp.where(one == pivot, 1.0, top[step : step + 1]) * scale
            gone = (spot[:width] == pivot) & (own_row > step)
            top = jnp.where(gone, 0.0, top) - upper * line
            if start + width < R:
                rest = rest - column[width:] * jnp.where(inside & (one > pivot), 0.0, line)
        pieces = [work[:start]] * (start > 0) + [top] + [rest] * (start + width < R)
        work = jnp.concatenate(pieces, axis=0)
        yield
    diag = jnp.where(spot == row, work, 0.0)
    scale = jnp.where(
        left,
        lax.rsqrt(jnp.sum(jnp.where(left, diag, 0.0), axis=1, keepdims=True)),
        lax.rsqrt(jnp.sum(jnp.where(left, 0.0, diag), axis=1, keepdims=True)),
    )
    work = jnp.where(spot < row, work * scale, jnp.where(spot == row, scale, 0.0))
    return jnp.concatenate([jnp.where(left, work, 0.0), jnp.where(left, 0.0, work)], axis=0)


def factor_pair(gram, beside):
    left = iota((R, LANES), 1) < R
    eye = unit()
    first, second, other = together(
        inverse_factor(jnp.where(left, gram, eye), 0),
        inverse_factor(jnp.where(left, eye, gram), R, down=False),
        beside,
    )
    turned = pltpu.roll(second, R, 1)
    zero = jnp.zeros((R, LANES), F32)
    inverse = jnp.concatenate(
        [jnp.where(left, pltpu.roll(first, R, 1), zero), jnp.where(left, zero, turned)], axis=0
    )
    return first, turned, inverse, other


def split_dot(left, right, contract):
    (high, low), (top, rest) = (three_terms(x)[:2] for x in (left, right))
    return dot(
        jnp.concatenate([high, high, low], axis=contract[0][0]),
        jnp.concatenate([top, rest, top], axis=contract[1][0]),
        contract,
    )


def unit():
    lane, row = iota((R, LANES), 1), iota((R, LANES), 0)
    return jnp.where((lane & (R - 1)) == row, 1.0, 0.0).astype(F32)


def grams(both):
    square = dot(both, both, ((0,), (0,)), HIGH)
    return jnp.where(iota((R, LANES), 1) < R, square[:R], square[R:])


def three_terms(value):
    high = value.astype(BF16)
    rest = value - high.astype(F32)
    middle = rest.astype(BF16)
    return [high, middle, (rest - middle.astype(F32)).astype(BF16)]


def sketch_panels(facts, chosen, panel, sigma, basis, coef, copies):
    def kernel(facts, chosen, near, sigma, basis, coef, sketched, shared, panel):
        k_count, rows, cols = panel.shape

        def history():
            row, col = iota((OO, OO), 0), iota((OO, OO), 1)
            inner = (row & 15) == (col >> 4)
            spread = jnp.where((row & 15) == (col & 15), 1.0, 0.0).astype(BF16)
            same = iota((NO, OO), 0) == (iota((NO, OO), 1) >> 4)
            groups = []
            for k in range(k_count):
                summed = dot(basis[...], sigma[k], ((1,), (0,)))
                yield
                summed = jnp.concatenate(three_terms(summed), axis=0)
                pairs = dot(summed, jnp.concatenate([coef[k]] * 3, axis=0), ((0,), (0,)))
                yield
                pairs = jnp.where(inner, pairs, 0.0).reshape(NO, NO, OO)
                groups += three_terms(jnp.sum(pairs, axis=1))
                yield
            laid = dot(jnp.concatenate(groups, axis=0), spread, ((1,), (0,)))
            yield
            lines = []
            for k in range(k_count):
                base = 3 * NO * k
                total = laid[base : base + NO] + laid[base + NO : base + 2 * NO]
                total = total + laid[base + 2 * NO : base + 3 * NO]
                line = jnp.sum(jnp.where(same, total, 0.0), axis=0, keepdims=True)
                lines += [line[:, :LANES], line[:, LANES:]]
            return lines

        keep = keep_mask(facts, rows, cols)
        zero = jnp.zeros((rows, cols), BF16)
        parts = []
        for k in range(k_count):
            masked = jnp.where(keep, near[k], zero)
            panel[k] = masked
            parts.append(dot(masked, chosen[...], ((1,), (0,))))
        both = jnp.where(iota((rows, LANES), 1) < R, parts[0], parts[1])
        sketched[...] = both

        gram = grams(both)
        lane, row = iota((R, LANES), 1), iota((R, LANES), 0)
        left = lane < R
        trace = jnp.sum(gram * unit(), axis=0, keepdims=True)
        half = lane[:1] < R
        shift = jnp.where(
            half,
            jnp.sum(jnp.where(half, trace, 0.0), axis=1, keepdims=True),
            jnp.sum(jnp.where(half, 0.0, trace), axis=1, keepdims=True),
        )
        shift = shift * (SHIFT / R) + TINY
        first, second, inverse, lines = factor_pair(gram + unit() * shift, history())
        corners = jnp.where(lane >= row, first, second)
        folded = jnp.where(left[: R // 2], corners[: R // 2], pltpu.roll(corners, R, 1)[R // 2 :])
        diag = jnp.sum(jnp.where(lane == row, second, 0.0), axis=0, keepdims=True)
        told = [folded, diag, shift] + lines + [jnp.zeros((2, LANES), F32)]
        told = three_terms(jnp.concatenate(told, axis=0))
        told = jnp.concatenate(told + [jnp.zeros((128 - 3 * TOLD, LANES), BF16)], axis=0)
        own = split_dot(inverse, both, ((1,), (1,))).astype(BF16)
        chunk = cols // copies
        halves = chunk // LANES
        for place in range(copies):
            shared[place, k_count * halves * R :] = told
        for k in range(k_count):
            terms = dot(own, panel[k], ((1,), (0,)))[k * R : (k + 1) * R].astype(BF16)
            for place in range(copies):
                for part in range(halves):
                    at = place * chunk + part * LANES
                    base = (k * halves + part) * R
                    shared[place, base : base + R] = terms[:, at : at + LANES]

    k_count, rows, cols = panel.shape
    smem = pl.BlockSpec(memory_space=pltpu.SMEM)
    vmem = pl.BlockSpec(memory_space=pltpu.VMEM)
    told_rows = k_count * R * (cols // copies // LANES) + 128
    return pl.pallas_call(
        kernel,
        out_shape=(
            jax.ShapeDtypeStruct((rows, LANES), F32),
            jax.ShapeDtypeStruct((copies, told_rows, LANES), BF16),
        ),
        in_specs=[smem] + [vmem] * 5,
        out_specs=(vmem, vmem),
        scratch_shapes=[pltpu.VMEM(panel.shape, BF16)],
        compiler_params=pltpu.CompilerParams(vmem_limit_bytes=20 << 20),
        name="sketch_panels",
    )(facts, chosen, panel, sigma, basis, coef)


def finish_panels(told, sketched, green, hamilton, chunk):
    def kernel(told, sketched, green, hamilton, next_green, ortho, right):
        k_count, copies = green.shape[0], told.shape[0]
        halves = chunk // LANES
        top = k_count * halves * R
        lane, row = iota((R, LANES), 1), iota((R, LANES), 0)
        left = lane < R
        factors, extra = [], jnp.zeros((TOLD - R // 2, LANES), F32)
        for place in range(copies):
            high, middle, low = (
                told[place, top + i * TOLD : top + (i + 1) * TOLD].astype(F32) for i in range(3)
            )
            value = high + middle + low
            extra = extra + value[R // 2 :]
            corners = value[: R // 2]
            turned = pltpu.roll(corners, R, 1)
            diag = pltpu.roll(value[R // 2 : R // 2 + 1], R, 1)
            upper = jnp.concatenate([corners, turned], axis=0)
            lower = jnp.concatenate([turned, corners], axis=0)
            lower = jnp.where(
                lane - R < row, lower, jnp.where(lane - R == row, diag, jnp.zeros_like(lower))
            )
            factors.append(jnp.where(left, jnp.where(lane >= row, upper, 0.0), lower))
        factors = jnp.concatenate(factors, axis=0)

        def beside():
            outer = (iota((NO, OO), 1) >> 4) == iota((NO, OO), 0)
            tile = jnp.where((iota((NO, OO), 1) & 15) == iota((NO, OO), 0), 1.0, 0.0).astype(F32)

            def square(line):
                return dot(jnp.where(outer, line, 0.0), tile, ((1,), (1,)), HIGH)

            rates = []
            for k in range(k_count):
                base = 2 + 2 * k
                line = jnp.concatenate([extra[base : base + 1], extra[base + 1 : base + 2]], axis=1)
                rates.append(square(line) * (1.0 / 256.0))
            states = [square(green[k : k + 1]) for k in range(k_count)]
            operators = [square(hamilton[k : k + 1]) for k in range(k_count)]
            yield
            for _ in range(2):
                pairs = [
                    (dot(h, g, ((1,), (0,)), HIGH), dot(g, h, ((1,), (0,)), HIGH))
                    for g, h in zip(states, operators)
                ]
                states = [
                    g + STEP * (left_prod - right_prod + rate)
                    for g, (left_prod, right_prod), rate in zip(states, pairs, rates)
                ]
                yield
            for k in range(k_count):
                flat = jnp.where(outer, dot(states[k], tile, ((1,), (0,)), HIGH), 0.0)
                next_green[k : k + 1] = jnp.sum(flat, axis=0, keepdims=True)
            yield
            first = factors.astype(BF16)
            second = (factors - first.astype(F32)).astype(BF16)
            sums = []
            for k in range(k_count):
                terms = [
                    jnp.concatenate(
                        [
                            told[place, (k * halves + part) * R : (k * halves + part + 1) * R]
                            for place in range(copies)
                        ],
                        axis=0,
                    )
                    for part in range(halves)
                ]
                terms = jnp.concatenate(terms, axis=1)
                both = dot(first, terms, ((0,), (0,))) + dot(second, terms, ((0,), (0,)))
                sums.append(both[k * R : (k + 1) * R])
                yield
            return jnp.concatenate(sums, axis=0)

        inverse, sums = together(
            inverse_pair(grams(factors) - unit() * extra[1:2]), beside()
        )
        coeffs = split_dot(inverse, sums, ((1,), (0,)))
        turned = split_dot(inverse, sketched[...], ((1,), (1,)))
        for k in range(k_count):
            right[k] = coeffs[k * R : (k + 1) * R]
            ortho[k] = turned[k * R : (k + 1) * R]

    k_count, rows = green.shape[0], sketched.shape[0]
    vmem = pl.BlockSpec(memory_space=pltpu.VMEM)
    return pl.pallas_call(
        kernel,
        out_shape=(
            jax.ShapeDtypeStruct((k_count, OO), F32),
            jax.ShapeDtypeStruct((k_count, R, rows), F32),
            jax.ShapeDtypeStruct((k_count, R, chunk), F32),
        ),
        in_specs=[vmem] * 4,
        out_specs=(vmem, vmem, vmem),
        compiler_params=pltpu.CompilerParams(vmem_limit_bytes=20 << 20),
        name="finish_panels",
    )(told, sketched, green, hamilton)


def body(
    sigma_history,
    time_basis,
    history_coef,
    green_now,
    hamilton,
    panel_block,
    panel_lengths,
    owners,
    sketch,
):
    ka_count, ta_count = lax.axis_size("ka"), lax.axis_size("ta")
    k_count = green_now.shape[0]
    assert NO * sigma_history.shape[1] * ta_count == 65536 and k_count == 2
    groups = [
        [place * ta_count + (group ^ turn(place)) for place in range(ka_count)]
        for group in range(ta_count)
    ]
    me = lax.axis_index("ta").astype(jnp.int32).reshape(1)
    asked = jnp.pad(owners.reshape(2), (0, LANES - 2)) + jnp.pad(panel_lengths, (2, LANES - 3))
    asked = asked + jnp.where(iota((1, LANES), 1)[0] == 3, me[0], 0)
    asked = jnp.broadcast_to(asked[None, None], (ka_count, 1, LANES))
    told = lax.all_to_all(
        asked,
        ("ka", "ta"),
        0,
        0,
        axis_index_groups=groups,
    ).reshape(ka_count, LANES)
    bring = (sigma_history, time_basis.T, history_coef, panel_block)
    picked, facts, sigma, basis, coef, panel = pick_rows(
        ka_count, ta_count, told, me, sketch, bring
    )
    chosen = lax.all_to_all(picked, "ka", 0, 0).reshape(-1, LANES)
    sketched, shared = sketch_panels(facts, chosen, panel, sigma, basis, coef, ta_count)
    told = lax.all_to_all(shared, "ta", 0, 0)
    chunk = panel_block.shape[2] // ta_count
    green_next, ortho, right = finish_panels(told, sketched, green_now, hamilton, chunk)
    return (green_next, ortho.transpose(0, 2, 1), right)


def solution(mesh):
    in_specs = (
        P("ka", "ta", None),
        P("ta", None),
        P("ka", "ta", None),
        P("ka", None),
        P("ka", None),
        P("ka", "ta", None),
        P("ta"),
        P("ka", None),
        P(None, "ka", None),
    )
    out_specs = (P("ka", None), P("ka", "ta", None), P("ka", None, "ta"))
    return jax.shard_map(body, mesh=mesh, in_specs=in_specs, out_specs=out_specs, check_vma=False)
```

```python
import jax
import jax.numpy as jnp
from jax import lax
from jax.experimental import pallas as pl
from jax.experimental.pallas import tpu as pltpu
from jax.sharding import PartitionSpec as P

NO = 16
OO = NO * NO
R = 64
SLOTS = 16
TOTAL = 120
LANES = 128
STEP = 0.25
BATCH = 8
TOLD = R // 2 + 8
SHIFT = 2.0**-12
TINY = 1e-30
HIGH = lax.Precision.HIGHEST
F32 = jnp.float32
BF16 = jnp.bfloat16


def turn(place):
    return place if place < 4 else 0


def dot(left, right, contract, precision=None):
    return lax.dot_general(
        left, right, (contract, ((), ())), precision=precision, preferred_element_type=F32
    )


def iota(shape, dim):
    return lax.broadcasted_iota(jnp.int32, shape, dim)


def pick_rows(ka_count, ta_count, told, me, sketch, bring):
    count = len(bring)

    def kernel(told, me, sketch_far, *refs):
        far, (picked, facts), near = refs[:count], refs[count : count + 2], refs[count + 2 :]
        near, (sketch, double, sem) = near[:count], near[count:]
        load = pltpu.make_async_copy(sketch_far, sketch, sem.at[count])
        load.start()
        loads = [pltpu.make_async_copy(far[i], near[i], sem.at[i]) for i in range(count)]
        for other in loads:
            other.start()
        before = jnp.int32(0)
        after = jnp.int32(0)
        length = jnp.int32(0)
        for place in range(4):
            where_from, amount = told[place, 3], told[place, 2]
            before = before + jnp.where(where_from < me[0], amount, 0)
            after = after + jnp.where(where_from >= me[0], amount, 0)
            length = length + jnp.where(where_from == me[0], amount, 0)
        facts[0] = jnp.where(me[0] < ta_count // 2, before, TOTAL - after)
        facts[1] = length
        load.wait()
        for rank in range(sketch.shape[0]):
            rows = sketch[rank]
            double[rank] = jnp.concatenate([rows, rows], axis=1)
        left = iota(double.shape[1:], 1) < R

        def one(place, carry):
            picked[place] = jnp.where(left, double[told[place, 0]], double[told[place, 1]])
            return carry

        lax.fori_loop(0, ka_count, one, 0, unroll=8)
        for other in loads:
            other.wait()

    ranks, rows, _ = sketch.shape
    smem = pl.BlockSpec(memory_space=pltpu.SMEM)
    vmem = pl.BlockSpec(memory_space=pltpu.VMEM)
    hbm = pl.BlockSpec(memory_space=pltpu.HBM)
    return pl.pallas_call(
        kernel,
        out_shape=(
            jax.ShapeDtypeStruct((ka_count, rows, LANES), BF16),
            jax.ShapeDtypeStruct((2,), jnp.int32),
        )
        + tuple(jax.ShapeDtypeStruct(x.shape, x.dtype) for x in bring),
        in_specs=[smem] * 2 + [hbm] * (1 + count),
        out_specs=(vmem, smem) + (vmem,) * count,
        scratch_shapes=[
            pltpu.VMEM(sketch.shape, BF16),
            pltpu.VMEM((ranks, rows, LANES), BF16),
            pltpu.SemaphoreType.DMA((count + 1,)),
        ],
        compiler_params=pltpu.CompilerParams(vmem_limit_bytes=8 << 20),
        name="pick_rows",
    )(told, me, *[pltpu.with_memory_space_constraint(x, pltpu.HBM) for x in (sketch, *bring)])


def keep_mask(facts, rows, cols):
    slot = iota((rows, 1), 0) >> 4
    top = jnp.where(slot < facts[1], facts[0] + slot + SLOTS // 2, -1)
    group = iota((1, cols), 1) >> 4
    return group.astype(F32).astype(BF16) <= top.astype(F32).astype(BF16)


def together(*stages):
    results, running = {}, dict(enumerate(stages))
    while running:
        for place, stage in list(running.items()):
            try:
                next(stage)
            except StopIteration as end:
                results[place] = end.value
                del running[place]
    return [results[place] for place in range(len(stages))]


def inverse_factor(work, offset, down=True):
    for batch in range(0, R, BATCH):
        order = [c if down else R - 1 - c for c in range(batch, batch + BATCH)]
        edge = (order[0] // 8) * 8
        low, high = (edge, R) if down else (0, edge + 8)
        part = work[low:high]
        rows = high - low
        place = low + iota((rows, LANES), 0)
        columns = [
            jnp.broadcast_to(part[:, offset + c : offset + c + 1], (rows, LANES)) for c in order
        ]
        for step, pivot in enumerate(order):
            at = pivot - low
            column = columns[step]
            scale = 1.0 / column[at : at + 1]
            rest = jnp.where(place > pivot if down else place < pivot, column, 0.0)
            for later in range(step + 1, BATCH):
                columns[later] = columns[later] - rest * (columns[later][at : at + 1] * scale)
            part = part - rest * (part[at : at + 1] * scale)
        pieces = [work[:low]] * (low > 0) + [part] + [work[high:]] * (high < R)
        work = pieces[0] if len(pieces) == 1 else jnp.concatenate(pieces, axis=0)
        yield
    lane, row = iota((R, LANES), 1), iota((R, LANES), 0)
    diag = jnp.sum(jnp.where(lane == row + offset, work, 0.0), axis=1, keepdims=True)
    return work * lax.rsqrt(diag)


def inverse_pair(work):
    width = 8
    spot = iota((R, LANES), 1) & (R - 1)
    row, left = iota((R, LANES), 0), iota((R, LANES), 1) < R
    one, own_row = spot[:1], row[:width]
    for start in range(0, R, width):
        top, rest = work[start : start + width], work[start + width :]
        part = work[start:]
        columns = [
            jnp.where(
                left[start:],
                jnp.broadcast_to(part[:, c : c + 1], part.shape),
                jnp.broadcast_to(part[:, R + c : R + c + 1], part.shape),
            )
            for c in range(start, start + width)
        ]
        inside = (one >= start) & (one < start + width)
        rest = jnp.where(inside, 0.0, rest)
        for step in range(width):
            pivot = start + step
            column = columns[step]
            scale = 1.0 / column[step : step + 1]
            upper = jnp.where(own_row > step, column[:width], 0.0)
            column = jnp.concatenate([upper, column[width:]], axis=0) if start + width < R else upper
            for later in range(step + 1, width):
                columns[later] = columns[later] - column * (columns[later][step : step + 1] * scale)
            line = jnp.where(one == pivot, 1.0, top[step : step + 1]) * scale
            gone = (spot[:width] == pivot) & (own_row > step)
            top = jnp.where(gone, 0.0, top) - upper * line
            if start + width < R:
                rest = rest - column[width:] * jnp.where(inside & (one > pivot), 0.0, line)
        pieces = [work[:start]] * (start > 0) + [top] + [rest] * (start + width < R)
        work = jnp.concatenate(pieces, axis=0)
        yield
    diag = jnp.where(spot == row, work, 0.0)
    scale = jnp.where(
        left,
        lax.rsqrt(jnp.sum(jnp.where(left, diag, 0.0), axis=1, keepdims=True)),
        lax.rsqrt(jnp.sum(jnp.where(left, 0.0, diag), axis=1, keepdims=True)),
    )
    work = jnp.where(spot < row, work * scale, jnp.where(spot == row, scale, 0.0))
    return jnp.concatenate([jnp.where(left, work, 0.0), jnp.where(left, 0.0, work)], axis=0)


def factor_pair(gram, beside):
    left = iota((R, LANES), 1) < R
    eye = unit()
    first, second, other = together(
        inverse_factor(jnp.where(left, gram, eye), 0),
        inverse_factor(jnp.where(left, eye, gram), R, down=False),
        beside,
    )
    turned = pltpu.roll(second, R, 1)
    zero = jnp.zeros((R, LANES), F32)
    inverse = jnp.concatenate(
        [jnp.where(left, pltpu.roll(first, R, 1), zero), jnp.where(left, zero, turned)], axis=0
    )
    return first, turned, inverse, other


def split_dot(left, right, contract):
    (high, low), (top, rest) = (three_terms(x)[:2] for x in (left, right))
    return dot(
        jnp.concatenate([high, high, low], axis=contract[0][0]),
        jnp.concatenate([top, rest, top], axis=contract[1][0]),
        contract,
    )


def unit():
    lane, row = iota((R, LANES), 1), iota((R, LANES), 0)
    return jnp.where((lane & (R - 1)) == row, 1.0, 0.0).astype(F32)


def grams(both):
    square = dot(both, both, ((0,), (0,)), HIGH)
    return jnp.where(iota((R, LANES), 1) < R, square[:R], square[R:])


def three_terms(value):
    high = value.astype(BF16)
    rest = value - high.astype(F32)
    middle = rest.astype(BF16)
    return [high, middle, (rest - middle.astype(F32)).astype(BF16)]


def sketch_panels(facts, chosen, panel, sigma, basis, coef, copies):
    def kernel(facts, chosen, near, *refs):
        far, (sketched, shared, panel), (sigma, basis, coef, sem) = refs[:3], refs[3:6], refs[6:]
        loads = [
            pltpu.make_async_copy(far[i], ref, sem.at[i])
            for i, ref in enumerate((sigma, basis, coef))
        ]
        for load in loads:
            load.start()
        k_count, rows, cols = panel.shape

        def history():
            row, col = iota((OO, OO), 0), iota((OO, OO), 1)
            inner = (row & 15) == (col >> 4)
            spread = jnp.where((row & 15) == (col & 15), 1.0, 0.0).astype(BF16)
            same = iota((NO, OO), 0) == (iota((NO, OO), 1) >> 4)
            groups = []
            for k in range(k_count):
                summed = dot(basis[...], sigma[k], ((1,), (0,)))
                yield
                summed = jnp.concatenate(three_terms(summed), axis=0)
                pairs = dot(summed, jnp.concatenate([coef[k]] * 3, axis=0), ((0,), (0,)))
                yield
                pairs = jnp.where(inner, pairs, 0.0).reshape(NO, NO, OO)
                groups += three_terms(jnp.sum(pairs, axis=1))
                yield
            laid = dot(jnp.concatenate(groups, axis=0), spread, ((1,), (0,)))
            yield
            lines = []
            for k in range(k_count):
                base = 3 * NO * k
                total = laid[base : base + NO] + laid[base + NO : base + 2 * NO]
                total = total + laid[base + 2 * NO : base + 3 * NO]
                line = jnp.sum(jnp.where(same, total, 0.0), axis=0, keepdims=True)
                lines += [line[:, :LANES], line[:, LANES:]]
            return lines

        keep = keep_mask(facts, rows, cols)
        zero = jnp.zeros((rows, cols), BF16)
        parts = []
        for k in range(k_count):
            masked = jnp.where(keep, near[k], zero)
            panel[k] = masked
            parts.append(dot(masked, chosen[...], ((1,), (0,))))
        both = jnp.where(iota((rows, LANES), 1) < R, parts[0], parts[1])
        sketched[...] = both

        for load in loads:
            load.wait()
        gram = grams(both)
        lane, row = iota((R, LANES), 1), iota((R, LANES), 0)
        left = lane < R
        trace = jnp.sum(gram * unit(), axis=0, keepdims=True)
        half = lane[:1] < R
        shift = jnp.where(
            half,
            jnp.sum(jnp.where(half, trace, 0.0), axis=1, keepdims=True),
            jnp.sum(jnp.where(half, 0.0, trace), axis=1, keepdims=True),
        )
        shift = shift * (SHIFT / R) + TINY
        first, second, inverse, lines = factor_pair(gram + unit() * shift, history())
        corners = jnp.where(lane >= row, first, second)
        folded = jnp.where(left[: R // 2], corners[: R // 2], pltpu.roll(corners, R, 1)[R // 2 :])
        diag = jnp.sum(jnp.where(lane == row, second, 0.0), axis=0, keepdims=True)
        told = [folded, diag, shift] + lines + [jnp.zeros((2, LANES), F32)]
        told = three_terms(jnp.concatenate(told, axis=0))
        told = jnp.concatenate(told + [jnp.zeros((128 - 3 * TOLD, LANES), BF16)], axis=0)
        own = split_dot(inverse, both, ((1,), (1,))).astype(BF16)
        chunk = cols // copies
        halves = chunk // LANES
        for place in range(copies):
            shared[place, k_count * halves * R :] = told
        for k in range(k_count):
            terms = dot(own, panel[k], ((1,), (0,)))[k * R : (k + 1) * R].astype(BF16)
            for place in range(copies):
                for part in range(halves):
                    at = place * chunk + part * LANES
                    base = (k * halves + part) * R
                    shared[place, base : base + R] = terms[:, at : at + LANES]

    k_count, rows, cols = panel.shape
    smem = pl.BlockSpec(memory_space=pltpu.SMEM)
    vmem = pl.BlockSpec(memory_space=pltpu.VMEM)
    told_rows = k_count * R * (cols // copies // LANES) + 128
    return pl.pallas_call(
        kernel,
        out_shape=(
            jax.ShapeDtypeStruct((rows, LANES), F32),
            jax.ShapeDtypeStruct((copies, told_rows, LANES), BF16),
        ),
        in_specs=[smem, vmem, vmem] + [pl.BlockSpec(memory_space=pltpu.HBM)] * 3,
        out_specs=(vmem, vmem),
        scratch_shapes=[pltpu.VMEM(x.shape, BF16) for x in (panel, sigma, basis, coef)]
        + [pltpu.SemaphoreType.DMA((3,))],
        compiler_params=pltpu.CompilerParams(vmem_limit_bytes=20 << 20),
        name="sketch_panels",
    )(
        facts,
        chosen,
        panel,
        *[pltpu.with_memory_space_constraint(x, pltpu.HBM) for x in (sigma, basis, coef)],
    )


def finish_panels(told, sketched, green, hamilton, chunk):
    def kernel(told, sketched, green, hamilton, next_green, ortho, right):
        k_count, copies = green.shape[0], told.shape[0]
        halves = chunk // LANES
        top = k_count * halves * R
        lane, row = iota((R, LANES), 1), iota((R, LANES), 0)
        left = lane < R
        factors, extra = [], jnp.zeros((TOLD - R // 2, LANES), F32)
        for place in range(copies):
            high, middle, low = (
                told[place, top + i * TOLD : top + (i + 1) * TOLD].astype(F32) for i in range(3)
            )
            value = high + middle + low
            extra = extra + value[R // 2 :]
            corners = value[: R // 2]
            turned = pltpu.roll(corners, R, 1)
            diag = pltpu.roll(value[R // 2 : R // 2 + 1], R, 1)
            upper = jnp.concatenate([corners, turned], axis=0)
            lower = jnp.concatenate([turned, corners], axis=0)
            lower = jnp.where(
                lane - R < row, lower, jnp.where(lane - R == row, diag, jnp.zeros_like(lower))
            )
            factors.append(jnp.where(left, jnp.where(lane >= row, upper, 0.0), lower))
        factors = jnp.concatenate(factors, axis=0)

        def beside():
            outer = (iota((NO, OO), 1) >> 4) == iota((NO, OO), 0)
            tile = jnp.where((iota((NO, OO), 1) & 15) == iota((NO, OO), 0), 1.0, 0.0).astype(F32)

            def square(line):
                return dot(jnp.where(outer, line, 0.0), tile, ((1,), (1,)), HIGH)

            rates = []
            for k in range(k_count):
                base = 2 + 2 * k
                line = jnp.concatenate([extra[base : base + 1], extra[base + 1 : base + 2]], axis=1)
                rates.append(square(line) * (1.0 / 256.0))
            states = [square(green[k : k + 1]) for k in range(k_count)]
            operators = [square(hamilton[k : k + 1]) for k in range(k_count)]
            yield
            for _ in range(2):
                pairs = [
                    (dot(h, g, ((1,), (0,)), HIGH), dot(g, h, ((1,), (0,)), HIGH))
                    for g, h in zip(states, operators)
                ]
                states = [
                    g + STEP * (left_prod - right_prod + rate)
                    for g, (left_prod, right_prod), rate in zip(states, pairs, rates)
                ]
                yield
            for k in range(k_count):
                flat = jnp.where(outer, dot(states[k], tile, ((1,), (0,)), HIGH), 0.0)
                next_green[k : k + 1] = jnp.sum(flat, axis=0, keepdims=True)
            yield
            first = factors.astype(BF16)
            second = (factors - first.astype(F32)).astype(BF16)
            sums = []
            for k in range(k_count):
                terms = [
                    jnp.concatenate(
                        [
                            told[place, (k * halves + part) * R : (k * halves + part + 1) * R]
                            for place in range(copies)
                        ],
                        axis=0,
                    )
                    for part in range(halves)
                ]
                terms = jnp.concatenate(terms, axis=1)
                both = dot(first, terms, ((0,), (0,))) + dot(second, terms, ((0,), (0,)))
                sums.append(both[k * R : (k + 1) * R])
                yield
            return jnp.concatenate(sums, axis=0)

        inverse, sums = together(
            inverse_pair(grams(factors) - unit() * extra[1:2]), beside()
        )
        coeffs = split_dot(inverse, sums, ((1,), (0,)))
        turned = split_dot(inverse, sketched[...], ((1,), (1,)))
        for k in range(k_count):
            right[k] = coeffs[k * R : (k + 1) * R]
            ortho[k] = turned[k * R : (k + 1) * R]

    k_count, rows = green.shape[0], sketched.shape[0]
    vmem = pl.BlockSpec(memory_space=pltpu.VMEM)
    return pl.pallas_call(
        kernel,
        out_shape=(
            jax.ShapeDtypeStruct((k_count, OO), F32),
            jax.ShapeDtypeStruct((k_count, R, rows), F32),
            jax.ShapeDtypeStruct((k_count, R, chunk), F32),
        ),
        in_specs=[vmem] * 4,
        out_specs=(vmem, vmem, vmem),
        compiler_params=pltpu.CompilerParams(vmem_limit_bytes=20 << 20),
        name="finish_panels",
    )(told, sketched, green, hamilton)


def body(
    sigma_history,
    time_basis,
    history_coef,
    green_now,
    hamilton,
    panel_block,
    panel_lengths,
    owners,
    sketch,
):
    ka_count, ta_count = lax.axis_size("ka"), lax.axis_size("ta")
    k_count = green_now.shape[0]
    assert NO * sigma_history.shape[1] * ta_count == 65536 and k_count == 2
    groups = [
        [place * ta_count + (group ^ turn(place)) for place in range(ka_count)]
        for group in range(ta_count)
    ]
    me = lax.axis_index("ta").astype(jnp.int32).reshape(1)
    asked = jnp.pad(owners.reshape(2), (0, LANES - 2)) + jnp.pad(panel_lengths, (2, LANES - 3))
    asked = asked + jnp.where(iota((1, LANES), 1)[0] == 3, me[0], 0)
    asked = jnp.broadcast_to(asked[None, None], (ka_count, 1, LANES))
    told = lax.all_to_all(
        asked,
        ("ka", "ta"),
        0,
        0,
        axis_index_groups=groups,
    ).reshape(ka_count, LANES)
    bring = (panel_block,)
    picked, facts, panel = pick_rows(
        ka_count, ta_count, told, me, sketch, bring
    )
    chosen = lax.all_to_all(picked, "ka", 0, 0).reshape(-1, LANES)
    sketched, shared = sketch_panels(
        facts, chosen, panel, sigma_history, time_basis.T, history_coef, ta_count
    )
    told = lax.all_to_all(shared, "ta", 0, 0)
    chunk = panel_block.shape[2] // ta_count
    green_next, ortho, right = finish_panels(told, sketched, green_now, hamilton, chunk)
    return (green_next, ortho.transpose(0, 2, 1), right)


def solution(mesh):
    in_specs = (
        P("ka", "ta", None),
        P("ta", None),
        P("ka", "ta", None),
        P("ka", None),
        P("ka", None),
        P("ka", "ta", None),
        P("ta"),
        P("ka", None),
        P(None, "ka", None),
    )
    out_specs = (P("ka", None), P("ka", "ta", None), P("ka", None, "ta"))
    return jax.shard_map(body, mesh=mesh, in_specs=in_specs, out_specs=out_specs, check_vma=False)
```
